128 devices in a mesh: row: 16 (over x, z), col: 8 (over y, core).
Axes of the slice: x: 4, y: 4, z: 4, core: 2. Of those that a mesh axis runs over, the one named last changes fastest.
Arguments:
- t_upper: bfloat16 [3, 4096, 4096], P(None, 'row', 'col'), may hold values from -0.03125 to 0.03125
- t_old: bfloat16 [3, 4096, 24576], P(None, 'row', 'col'), may hold values from -0.03125 to 0.03125
- inverses: bfloat16 [3, 4096, 4096], P(None, 'row', 'col'), may hold values from -1 to 1.5, as said below
- forcing: float32 [3, 4096, 128], P(None, 'row'), may hold values from -6 to 6
- x_old: bfloat16 [24576, 128], P('col'), may hold values from -6 to 6
- offsets: float32 [128], replicated, may hold values from -0.5 to 0.5
- starts: int32 [128], replicated, may hold values from 0 to 36864
- column_map: int32 [128], replicated, may hold values from 0 to 127, each once
- z_cols: bfloat16 [49152, 3, 4096], P('row', None, 'col'), may hold values from -0.0546875 to 0.0546875
- acc: float32 [49152, 128], P(('row', 'col')), may hold values from -6 to 6
Outputs:
- solved: float32 [3, 4096, 128], P(None, ('row', 'col'))
- acc_out: float32 [49152, 128], P(('row', 'col'))
The draws below stay inside these ranges and needn't reach their ends.
Inputs may be any that keep to these rules, and one draw needn't show every extreme that they name: `inverses`: dense matrices with a dominant positive diagonal.
All inputs are finite; a program needn't handle non-finite values.
Results may differ from the reference program's by a relative error of at most 0.0003.
Values may be sent and summed in bfloat16 or wider, within the bound.
No kernel may reach another device: no remote copies, remote signals or barrier semaphores. Data moves between devices by JAX's collectives and lax.ppermute only.
A program may use at most 128 MiB of HBM per device.

```python
import jax
import jax.numpy as jnp
from jax import lax

B = 4096
STEPS = 3
NEUMANN = 3
E = 128
K = 24576
NZ = 49152


def draw_inverses(key, part):
    key_diag = jax.random.fold_in(key, 11)
    key_off = jax.random.fold_in(key, 12)
    diag = jnp.exp(jax.random.uniform(key_diag, (STEPS, B), jnp.float32, jnp.log(0.5), 0.0))
    spread = jax.random.normal(key_off, (STEPS, B, B), jnp.float32) * (0.3 / B ** 0.5)
    eye = jnp.eye(B, dtype=jnp.float32)
    whole = spread + diag[:, :, None] * eye[None, :, :]
    return jnp.clip(whole, -1.0, 1.5).astype(jnp.bfloat16)


def touch_ends(entries, stream_key, low, largest):
    index_at = [jax.random.randint(jax.random.fold_in(stream_key, axis), (), 0, length) for axis, length in enumerate(entries.shape)]
    widest = entries.shape.index(max(entries.shape))
    next_to = index_at[:widest] + [(index_at[widest] + 1) % entries.shape[widest]] + index_at[widest + 1:]
    return entries.at[tuple(index_at)].set(low).at[tuple(next_to)].set(largest)


def level_of(rng, extent, split, low, largest):
    loudness, own = 1.0, jax.random.fold_in(rng, 6)
    for dim, blocks in split:
        steps = jnp.exp(jax.random.uniform(jax.random.fold_in(own, dim), (blocks,), jnp.float32, low / len(split), largest / len(split)))
        loudness = loudness * jnp.repeat(steps, extent[dim] // blocks).reshape([-1 if axis == dim else 1 for axis in range(len(extent))])
    return loudness


def normal_values(stream_key, shape, scale, most, cuts=(), kind=jnp.bfloat16):
    result = scale * jax.random.normal(stream_key, shape, jnp.float32)
    if cuts:
        result = result * level_of(stream_key, shape, cuts, -0.22, 0.18)
    return jnp.clip(result, -most, most).astype(kind)


def setup_inputs(seed: int = 0) -> dict:
    keys = jax.random.split(jax.random.key(seed), 11)
    return {
        "t_upper": normal_values(keys[0], (3, B, B), (2 * B + K) ** -0.5, 0.03125, ((1, 16), (2, 8))),
        "t_old": normal_values(keys[1], (STEPS, B, K), (2 * B + K) ** -0.5, 0.03125, ((1, 16), (2, 8))),
        "inverses": draw_inverses(jax.random.fold_in(keys[10], 71), 0),
        "forcing": normal_values(keys[3], (STEPS, B, E), 1.0, 6.0, ((1, 16),), jnp.float32),
        "x_old": normal_values(keys[4], (K, E), 1.0, 6.0, ((0, 8),)),
        "offsets": jnp.clip(jax.random.uniform(keys[5], (E,), jnp.float32, -0.5, 0.5), -0.5, 0.5),
        "starts": touch_ends(jax.random.randint(keys[6], (E,), 0, STEPS * B + K + 1), jax.random.fold_in(keys[6], 1), 0, STEPS * B + K).astype(jnp.int32),
        "column_map": jax.random.permutation(keys[7], E).astype(jnp.int32),
        "z_cols": normal_values(keys[8], (NZ, STEPS, B), (STEPS * B) ** -0.5, 0.0546875, ((0, 16), (2, 8))),
        "acc": normal_values(keys[9], (NZ, E), 1.0, 6.0, ((0, 128),), jnp.float32),
    }


def split_pair(values):
    upper = values.astype(jnp.bfloat16)
    lower = (values - lax.optimization_barrier(upper).astype(jnp.float32)).astype(jnp.bfloat16)
    return jnp.concatenate([upper, lower], axis=-1)


def fold_pair(product):
    return product[:, :E] + product[:, E:]


def reference(t_upper, t_old, inverses, forcing, x_old, offsets, starts, column_map, z_cols, acc):
    pairs = {}
    count = 0
    for first in range(STEPS):
        for second in range(first + 1, STEPS):
            pairs[(first, second)] = count
            count = count + 1
    old_rows = STEPS * B + jnp.arange(K, dtype=jnp.int32)
    old_live = old_rows[:, None] < starts[None, :]
    old_vals = jnp.where(old_live, x_old, jnp.zeros_like(x_old))
    results = [None] * STEPS
    rounded = [None] * STEPS
    for step in reversed(range(STEPS)):
        rhs = forcing[step] - jnp.dot(t_old[step], old_vals, preferred_element_type=jnp.float32)
        for later in range(step + 1, STEPS):
            rhs = rhs - fold_pair(jnp.dot(t_upper[pairs[(step, later)]], rounded[later], preferred_element_type=jnp.float32))
        term = fold_pair(jnp.dot(inverses[step], split_pair(rhs), preferred_element_type=jnp.float32))
        total = term
        for extra in range(1, NEUMANN):
            term = fold_pair(jnp.dot(inverses[step], split_pair(term), preferred_element_type=jnp.float32)) * offsets[None, :]
            total = total + term
        rows = step * B + jnp.arange(B, dtype=jnp.int32)
        total = jnp.where(rows[:, None] < starts[None, :], total, jnp.zeros_like(total))
        results[step] = total
        rounded[step] = split_pair(total)
    stacked = jnp.stack(rounded)
    index = jnp.concatenate([column_map, column_map + E]).astype(jnp.int32)
    picked = stacked[:, :, index].reshape(STEPS * B, 2 * E)
    contribution = fold_pair(jnp.dot(z_cols.reshape(NZ, STEPS * B), picked, preferred_element_type=jnp.float32))
    return jnp.stack(results), acc + contribution
```

```python
import jax
import jax.numpy as jnp
from jax import lax
from jax.sharding import PartitionSpec as P

NEUMANN = 3


def split_pair(values):
    upper = values.astype(jnp.bfloat16)
    lower = (values - lax.optimization_barrier(upper).astype(jnp.float32)).astype(jnp.bfloat16)
    return jnp.concatenate([upper, lower], axis=0)


def body(t_upper, t_old, inverses, forcing, x_old, offsets, starts, column_map, z_cols, acc):
    n_col = lax.axis_size("col")
    n_row = lax.axis_size("row")
    row_idx = lax.axis_index("row")
    col_idx = lax.axis_index("col")
    steps, row_block, width = forcing.shape
    col_block = t_upper.shape[2]
    old_cols = x_old.shape[0]
    full_rows = col_block * n_col
    group = width // n_col
    share = row_block // n_col

    inv_last = lax.all_gather(inverses[2], "col", axis=1, tiled=True)
    second = lax.all_gather(
        jnp.stack([t_upper[2], inverses[1]]), "col", axis=2, tiled=True
    )
    third = lax.all_gather(
        jnp.concatenate([t_upper[:2], inverses[:1]]), "col", axis=2, tiled=True
    )
    inv = {2: inv_last, 1: second[1], 0: third[2]}
    upper_of = {(1, 2): second[0], (0, 1): third[0], (0, 2): third[1]}

    def own_group(values):
        return lax.dynamic_slice_in_dim(values, col_idx * group, group, 0)

    my_starts = own_group(starts)[:, None]
    my_offsets = own_group(offsets)[:, None]

    old_rows = steps * full_rows + col_idx * old_cols + jnp.arange(old_cols, dtype=jnp.int32)
    old_vals = jnp.where(old_rows[:, None] < starts[None, :], x_old, jnp.zeros_like(x_old))
    old_part = lax.dot_general(
        old_vals,
        t_old.reshape(steps * row_block, old_cols),
        (((0,), (1,)), ((), ())),
        preferred_element_type=jnp.float32,
    )
    old_part = lax.all_to_all(
        old_part.reshape(n_col, group, steps * row_block), "col", 0, 0
    ).sum(0)
    forcing_t = lax.dynamic_slice_in_dim(
        forcing.reshape(steps * row_block, width), col_idx * group, group, 1
    ).T
    rhs_all = forcing_t - old_part

    def spread(values):
        pair = split_pair(values)
        got = lax.all_to_all(
            jnp.broadcast_to(pair[None], (n_row, *pair.shape)), "row", 0, 0
        )
        return jnp.swapaxes(got, 0, 1).reshape(2 * group, full_rows)

    def product(matrix, pairs):
        out = lax.dot_general(
            pairs, matrix, (((1,), (1,)), ((), ())), preferred_element_type=jnp.float32
        )
        return out[:group] + out[group:]

    whole = {}
    own = {}
    for step in reversed(range(steps)):
        rhs = rhs_all[:, step * row_block : (step + 1) * row_block]
        for later in range(step + 1, steps):
            rhs = rhs - product(upper_of[step, later], whole[later])
        term = product(inv[step], spread(rhs))
        total = term
        for extra in range(1, NEUMANN):
            term = product(inv[step], spread(term)) * my_offsets
            total = total + term
        rows = step * full_rows + row_idx * row_block + jnp.arange(row_block, dtype=jnp.int32)
        total = jnp.where(rows[None, :] < my_starts, total, jnp.zeros_like(total))
        own[step] = total
        whole[step] = spread(total)

    mine = jnp.stack([own[step] for step in range(steps)])
    solved = lax.all_gather(mine, "col", axis=1, tiled=True)
    solved = lax.dynamic_slice_in_dim(solved, col_idx * share, share, 2)
    solved = jnp.swapaxes(solved, 1, 2)

    send = jnp.stack([whole[step].reshape(2 * group, n_col, col_block) for step in range(steps)])
    send = jnp.transpose(send, (2, 0, 1, 3))
    got = lax.all_to_all(send, "col", 0, 0)
    got = got.reshape(n_col, steps, 2, group, col_block)
    got = jnp.transpose(got, (2, 0, 3, 1, 4)).reshape(2, width, steps * col_block)
    one_hot = (jnp.arange(width, dtype=jnp.int32)[:, None] == column_map[None, :]).astype(
        jnp.bfloat16
    )
    picked = [
        lax.dot_general(
            got[half], one_hot, (((0,), (0,)), ((), ())), preferred_element_type=jnp.float32
        ).astype(jnp.bfloat16)
        for half in range(2)
    ]
    picked = jnp.concatenate(picked, axis=1)
    z_rows = z_cols.shape[0]
    product_z = jnp.dot(
        z_cols.reshape(z_rows, steps * col_block), picked, preferred_element_type=jnp.float32
    )
    part = product_z[:, :width] + product_z[:, width:]
    part = lax.all_to_all(part.reshape(n_col, z_rows // n_col, width), "col", 0, 0).sum(0)
    return (solved, acc + part)


def solution(mesh):
    placed = (
        P(None, "row", "col"),
        P(None, "row", "col"),
        P(None, "row", "col"),
        P(None, "row", None),
        P("col", None),
        P(),
        P(),
        P(),
        P("row", None, "col"),
        P(("row", "col"), None),
    )
    return jax.shard_map(
        body,
        mesh=mesh,
        in_specs=placed,
        out_specs=(P(None, ("row", "col"), None), P(("row", "col"), None)),
        check_vma=False,
    )
```

```python
import functools

import jax
import jax.numpy as jnp
from jax import lax
from jax.experimental import pallas as pl
from jax.experimental.pallas import tpu as pltpu
from jax.sharding import PartitionSpec as P

NEUMANN = 3
F32 = jnp.float32
BF16 = jnp.bfloat16
VMEM_LIMIT = 16 << 20


def rows_product(pairs_ref, rows_ref, which):
    blocks, _, width = pairs_ref.shape
    per = blocks // rows_ref.shape[0]
    out = None
    for block in range(blocks):
        first = (block % per) * width
        part = lax.dot_general(
            pairs_ref[block],
            rows_ref[block // per, which, :, first : first + width],
            (((1,), (1,)), ((), ())),
            preferred_element_type=F32,
        )
        out = part if out is None else out + part
    half = out.shape[0] // 2
    return out[:half] + out[half:]


def pair_of(values):
    upper = values.astype(BF16)
    lower = (values - upper.astype(F32)).astype(BF16)
    return jnp.concatenate([upper, lower], axis=0)


def send_to_all(send_ref, pair):
    for peer in range(send_ref.shape[0]):
        send_ref[peer] = pair


def first_kernel(step, parts_ref, forcing_ref, rhs_ref, send_ref):
    width = send_ref.shape[2]
    rhs = forcing_ref[...] - jnp.sum(parts_ref[...], axis=0)
    rhs_ref[...] = rhs
    send_to_all(send_ref, pair_of(rhs[:, step * width : (step + 1) * width]))


def rhs_kernel(step, uses, *refs):
    rhs_ref, send_ref = refs[-2:]
    width = send_ref.shape[2]
    rhs = rhs_ref[:, step * width : (step + 1) * width]
    for k, which in enumerate(uses):
        rhs = rhs - rows_product(refs[2 * k], refs[2 * k + 1], which)
    send_to_all(send_ref, pair_of(rhs))


def first_term_kernel(which, pairs_ref, rows_ref, send_ref, total_ref):
    term = rows_product(pairs_ref, rows_ref, which)
    total_ref[...] = term
    send_to_all(send_ref, pair_of(term))


def next_term_kernel(which, pairs_ref, rows_ref, scale_ref, old_ref, send_ref, total_ref):
    term = rows_product(pairs_ref, rows_ref, which) * scale_ref[...]
    total_ref[...] = old_ref[...] + term
    send_to_all(send_ref, pair_of(term))


def last_term_kernel(which, pairs_ref, rows_ref, scale_ref, old_ref, limit_ref, send_ref, own_ref):
    term = rows_product(pairs_ref, rows_ref, which) * scale_ref[...]
    total = old_ref[...] + term
    row = lax.broadcasted_iota(jnp.int32, total.shape, 1)
    pair = pair_of(jnp.where(row < limit_ref[...], total, 0.0))
    own_ref[...] = pair
    send_to_all(send_ref, pair)


def columns_kernel(steps, *refs):
    send_ref = refs[-1]
    n_col = send_ref.shape[0]
    lanes = 128
    for step in range(steps):
        whole_ref, own_ref = refs[2 * step], refs[2 * step + 1]
        blocks, _, width = whole_ref.shape
        per = blocks // n_col
        share = width // n_col
        for col in range(n_col):
            for k in range(per):
                send_ref[col, step, :, k * width : (k + 1) * width] = whole_ref[col * per + k]
            first = col * share // lanes * lanes
            send_ref[col, step, :, per * width :] = own_ref[:, first : first + lanes]


def z_first_kernel(place_ref, got_ref, hot_ref, z_ref, out_ref, picked_ref):
    steps, _, depth = z_ref.shape

    @pl.when(pl.program_id(0) == 0)
    def _():
        for step in range(steps):
            whole = jnp.concatenate(
                [got_ref[k, step, :, :depth] for k in range(got_ref.shape[0])], axis=0
            )
            picked_ref[step] = lax.dot_general(
                whole, hot_ref[...], (((0,), (0,)), ((), ())), preferred_element_type=F32
            ).astype(BF16)

    z_tile(z_ref, picked_ref, out_ref)


def z_next_kernel(place_ref, picked_ref, z_ref, out_ref):
    z_tile(z_ref, picked_ref, out_ref)


def z_tile(z_ref, picked_ref, out_ref):
    out = None
    for step in range(z_ref.shape[0]):
        part = jnp.dot(z_ref[step], picked_ref[step], preferred_element_type=F32)
        out = part if out is None else out + part
    half = out.shape[1] // 2
    out_ref[0] = out[:, :half] + out[:, half:]


def call(kernel, outs, *args, flops=0):
    size = sum(a.size * a.dtype.itemsize for a in args)
    return pl.pallas_call(
        kernel,
        out_shape=outs,
        in_specs=[pl.BlockSpec(memory_space=pltpu.VMEM)] * len(args),
        out_specs=[pl.BlockSpec(memory_space=pltpu.VMEM)] * len(outs),
        compiler_params=pltpu.CompilerParams(vmem_limit_bytes=VMEM_LIMIT),
        cost_estimate=pl.CostEstimate(flops=flops, bytes_accessed=size, transcendentals=0),
    )(*args)


def in_vmem(values):
    return pltpu.with_memory_space_constraint(values, pltpu.VMEM)


def body(t_upper, t_old, inverses, forcing, x_old, offsets, starts, column_map, z_cols, acc):
    n_col = lax.axis_size("col")
    n_row = lax.axis_size("row")
    row_idx = lax.axis_index("row")
    col_idx = lax.axis_index("col")
    steps, row_block, width = forcing.shape
    col_block = t_upper.shape[2]
    old_cols = x_old.shape[0]
    full_rows = col_block * n_col
    group = width // n_col
    share = row_block // n_col
    shape = jax.ShapeDtypeStruct

    gather = functools.partial(lax.all_gather, axis_name="col", axis=0)
    set_a = gather(inverses[2:3])
    set_b = gather(jnp.concatenate([t_upper[2:3], inverses[1:2]]))
    set_c = gather(jnp.concatenate([t_upper[:2], inverses[:1]]))
    inv = {2: (set_a, 0), 1: (set_b, 1), 0: (set_c, 2)}
    upper_of = {(1, 2): (set_b, 0), (0, 1): (set_c, 0), (0, 2): (set_c, 1)}

    def own_group(values):
        return lax.dynamic_slice_in_dim(values, col_idx * group, group, 0)

    my_starts = own_group(starts)[:, None]
    my_offsets = own_group(offsets)[:, None]

    old_rows = steps * full_rows + col_idx * old_cols + jnp.arange(old_cols, dtype=jnp.int32)
    old_vals = jnp.where(old_rows[:, None] < starts[None, :], x_old, jnp.zeros_like(x_old))
    old_part = lax.dot_general(
        old_vals,
        t_old.reshape(steps * row_block, old_cols),
        (((0,), (1,)), ((), ())),
        preferred_element_type=F32,
    )
    old_part = lax.all_to_all(old_part.reshape(n_col, group, steps * row_block), "col", 0, 0)
    forcing_t = lax.dynamic_slice_in_dim(
        forcing.reshape(steps * row_block, width), col_idx * group, group, 1
    ).T

    send_shape = shape((n_row, 2 * group, row_block), BF16)
    vec_shape = shape((group, row_block), F32)
    own_shape = shape((2 * group, row_block), BF16)
    flops = 4 * group * row_block * full_rows

    def spread(send):
        return lax.all_to_all(send, "row", 0, 0)

    rhs_all, send = call(
        functools.partial(first_kernel, steps - 1),
        [shape((group, steps * row_block), F32), send_shape],
        old_part,
        forcing_t,
    )
    whole = {}
    own = {}
    for step in reversed(range(steps)):
        if step < steps - 1:
            args = []
            uses = []
            for later in range(step + 1, steps):
                rows, which = upper_of[step, later]
                args += [whole[later], in_vmem(rows)]
                uses.append(which)
            (send,) = call(
                functools.partial(rhs_kernel, step, uses),
                [send_shape],
                *args,
                rhs_all,
                flops=flops * len(uses),
            )
        rows, which = inv[step]
        rows = in_vmem(rows)
        send, total = call(
            functools.partial(first_term_kernel, which),
            [send_shape, vec_shape],
            spread(send),
            rows,
            flops=flops,
        )
        for extra in range(1, NEUMANN):
            if extra < NEUMANN - 1:
                send, total = call(
                    functools.partial(next_term_kernel, which),
                    [send_shape, vec_shape],
                    spread(send),
                    rows,
                    my_offsets,
                    total,
                    flops=flops,
                )
            else:
                limit = my_starts - (step * full_rows + row_idx * row_block)
                send, own[step] = call(
                    functools.partial(last_term_kernel, which),
                    [send_shape, own_shape],
                    spread(send),
                    rows,
                    my_offsets,
                    total,
                    limit,
                    flops=flops,
                )
        whole[step] = spread(send)

    lanes = 128
    args = []
    for step in range(steps):
        args += [whole[step], own[step]]
    (send,) = call(
        functools.partial(columns_kernel, steps),
        [shape((n_col, steps, 2 * group, col_block + lanes), BF16)],
        *args,
    )
    got = lax.all_to_all(send, "col", 0, 0)

    mine = lax.dynamic_slice_in_dim(
        got, col_block + col_idx % (lanes // share) * share, share, 3
    ).astype(F32)
    mine = mine[:, :, :group] + mine[:, :, group:]
    solved = jnp.transpose(mine, (1, 3, 0, 2)).reshape(steps, share, width)

    order = jnp.arange(2 * width, dtype=jnp.int32)
    half_of = order // group % 2
    value_of = order // (2 * group) * group + order % group
    target = jnp.concatenate([column_map, column_map + width])
    hot = ((half_of * width + value_of)[:, None] == target[None, :]).astype(BF16)

    z_rows = z_cols.shape[0]
    z_block = z_rows // n_col
    z_t = jnp.transpose(z_cols, (1, 0, 2))
    core = col_idx % 2
    z_spec = pl.BlockSpec((steps, z_block, col_block), lambda i, place: (0, 2 * i + place[0], 0))
    out_spec = pl.BlockSpec((1, z_block, width), lambda i, place: (i, 0, 0))
    z_params = pltpu.CompilerParams(vmem_limit_bytes=VMEM_LIMIT)
    cost = pl.CostEstimate(
        flops=2 * z_rows * steps * col_block * width,
        bytes_accessed=z_cols.size,
        transcendentals=0,
    )
    part_shape = shape((n_col // 2, z_block, width), F32)
    picked_shape = shape((steps, col_block, 2 * width), BF16)

    def fixed(array_shape):
        return pl.BlockSpec(array_shape, lambda i, place: (0,) * len(array_shape))

    theirs, picked = pl.pallas_call(
        z_first_kernel,
        out_shape=[part_shape, picked_shape],
        grid_spec=pltpu.PrefetchScalarGridSpec(
            num_scalar_prefetch=1,
            grid=(n_col // 2,),
            in_specs=[fixed(got.shape), fixed(hot.shape), z_spec],
            out_specs=[out_spec, fixed(picked_shape.shape)],
        ),
        compiler_params=z_params,
        cost_estimate=cost,
    )((1 - core)[None], got, hot, z_t)
    swapped = lax.ppermute(theirs, "col", [(i, i ^ 1) for i in range(n_col)])
    (ours,) = pl.pallas_call(
        z_next_kernel,
        out_shape=[part_shape],
        grid_spec=pltpu.PrefetchScalarGridSpec(
            num_scalar_prefetch=1,
            grid=(n_col // 2,),
            in_specs=[fixed(picked_shape.shape), z_spec],
            out_specs=[out_spec],
        ),
        compiler_params=z_params,
        cost_estimate=cost,
    )(core[None], picked, z_t)
    part = lax.all_to_all(
        ours + swapped,
        "col",
        0,
        0,
        axis_index_groups=[list(range(c, n_col, 2)) for c in range(2)],
    )
    return (solved, acc + part.sum(0))


def solution(mesh):
    placed = (
        P(None, "row", "col"),
        P(None, "row", "col"),
        P(None, "row", "col"),
        P(None, "row", None),
        P("col", None),
        P(),
        P(),
        P(),
        P("row", None, "col"),
        P(("row", "col"), None),
    )
    return jax.shard_map(
        body,
        mesh=mesh,
        in_specs=placed,
        out_specs=(P(None, ("row", "col"), None), P(("row", "col"), None)),
        check_vma=False,
    )
```

```python
import functools

import jax
import jax.numpy as jnp
from jax import lax
from jax.experimental import pallas as pl
from jax.experimental.pallas import tpu as pltpu
from jax.sharding import PartitionSpec as P

NEUMANN = 3
F32 = jnp.float32
BF16 = jnp.bfloat16
VMEM_LIMIT = 16 << 20
LANES = 128
CHUNK = 512


def rows_product(pairs_ref, rows_ref, which):
    blocks, _, width = pairs_ref.shape
    per = blocks // rows_ref.shape[0]
    out = None
    for block in range(blocks):
        first = (block % per) * width
        part = lax.dot_general(
            pairs_ref[block],
            rows_ref[block // per, which, :, first : first + width],
            (((1,), (1,)), ((), ())),
            preferred_element_type=F32,
        )
        out = part if out is None else out + part
    half = out.shape[0] // 2
    return out[:half] + out[half:]


def pair_of(values):
    upper = values.astype(BF16)
    lower = (values - upper.astype(F32)).astype(BF16)
    return jnp.concatenate([upper, lower], axis=0)


def send_to_all(send_ref, pair):
    for peer in range(send_ref.shape[0]):
        send_ref[peer] = pair


def first_kernel(step, parts_ref, forcing_ref, rhs_ref, send_ref):
    width = send_ref.shape[2]
    rhs = forcing_ref[...] - jnp.sum(parts_ref[...], axis=0)
    rhs_ref[...] = rhs
    send_to_all(send_ref, pair_of(rhs[:, step * width : (step + 1) * width]))


def rhs_kernel(step, uses, *refs):
    rhs_ref, send_ref = refs[-2:]
    width = send_ref.shape[2]
    rhs = rhs_ref[:, step * width : (step + 1) * width]
    for k, which in enumerate(uses):
        rhs = rhs - rows_product(refs[2 * k], refs[2 * k + 1], which)
    send_to_all(send_ref, pair_of(rhs))


def first_term_kernel(which, pairs_ref, rows_ref, send_ref, total_ref):
    term = rows_product(pairs_ref, rows_ref, which)
    total_ref[...] = term
    send_to_all(send_ref, pair_of(term))


def next_term_kernel(which, pairs_ref, rows_ref, scale_ref, old_ref, send_ref, total_ref):
    term = rows_product(pairs_ref, rows_ref, which) * scale_ref[...]
    total_ref[...] = old_ref[...] + term
    send_to_all(send_ref, pair_of(term))


def last_term_kernel(which, pairs_ref, rows_ref, scale_ref, old_ref, limit_ref, send_ref, own_ref):
    term = rows_product(pairs_ref, rows_ref, which) * scale_ref[...]
    total = old_ref[...] + term
    row = lax.broadcasted_iota(jnp.int32, total.shape, 1)
    pair = pair_of(jnp.where(row < limit_ref[...], total, 0.0))
    own_ref[...] = pair
    send_to_all(send_ref, pair)


def columns_kernel(whole_ref, own_ref, send_ref):
    n_col = send_ref.shape[0]
    blocks, _, width = whole_ref.shape
    per = blocks // n_col
    share = width // n_col
    for col in range(n_col):
        for k in range(per):
            send_ref[col, :, k * width : (k + 1) * width] = whole_ref[col * per + k]
        first = col * share // LANES * LANES
        send_ref[col, :, per * width :] = own_ref[:, first : first + LANES]


def pick(blocks, hot_ref):
    return lax.dot_general(
        jnp.concatenate(blocks, axis=0),
        hot_ref[...],
        (((0,), (0,)), ((), ())),
        preferred_element_type=F32,
    ).astype(BF16)


def fold(product):
    half = product.shape[1] // 2
    return product[:, :half] + product[:, half:]


def z_early_kernel(*refs):
    hot_ref, z_ref, out_ref, picked_ref = refs[-4:]
    gots = refs[:-4]

    @pl.when(pl.program_id(0) == 0)
    def _():
        for k, got_ref in enumerate(gots):
            cols, per, _, width = got_ref.shape
            for j in range(per):
                blocks = [got_ref[col, j] for col in range(cols)]
                picked_ref[k, j * width : (j + 1) * width] = pick(blocks, hot_ref)

    out = None
    for k in range(len(gots)):
        part = jnp.dot(z_ref[k], picked_ref[k], preferred_element_type=F32)
        out = part if out is None else out + part
    out_ref[0] = fold(out)


def z_first_kernel(place_ref, got_ref, hot_ref, z_ref, early_ref, out_ref, picked_ref):
    depth = z_ref.shape[2]

    @pl.when(pl.program_id(0) == 0)
    def _():
        blocks = [got_ref[k, :, :depth] for k in range(got_ref.shape[0])]
        picked_ref[...] = pick(blocks, hot_ref)

    z_next_kernel(place_ref, picked_ref, z_ref, early_ref, out_ref)


def z_next_kernel(place_ref, picked_ref, z_ref, early_ref, out_ref):
    product = jnp.dot(z_ref[0], picked_ref[...], preferred_element_type=F32)
    out_ref[0] = early_ref[0] + fold(product)


def old_kernel(base_ref, t_ref, old_ref, starts_ref, out_ref, sum_ref):
    k = pl.program_id(0)
    chunk = old_ref.shape[0]
    row = base_ref[0] + k * chunk + lax.broadcasted_iota(jnp.int32, old_ref.shape, 0)
    old = jnp.where(row < starts_ref[...], old_ref[...].astype(F32), 0.0).astype(BF16)
    part = jnp.concatenate(
        [
            lax.dot_general(
                old, t_ref[step], (((0,), (1,)), ((), ())), preferred_element_type=F32
            )
            for step in range(t_ref.shape[0])
        ],
        axis=1,
    )

    @pl.when(k == 0)
    def _():
        sum_ref[...] = part

    @pl.when(k > 0)
    def _():
        sum_ref[...] += part

    @pl.when(k == pl.num_programs(0) - 1)
    def _():
        group = out_ref.shape[1]
        for col in range(out_ref.shape[0]):
            out_ref[col] = sum_ref[col * group : (col + 1) * group]


def call(kernel, outs, *args, flops=0):
    size = sum(a.size * a.dtype.itemsize for a in args)
    return pl.pallas_call(
        kernel,
        out_shape=outs,
        in_specs=[pl.BlockSpec(memory_space=pltpu.VMEM)] * len(args),
        out_specs=[pl.BlockSpec(memory_space=pltpu.VMEM)] * len(outs),
        compiler_params=pltpu.CompilerParams(vmem_limit_bytes=VMEM_LIMIT),
        cost_estimate=pl.CostEstimate(flops=flops, bytes_accessed=size, transcendentals=0),
    )(*args)


def in_vmem(values):
    return pltpu.with_memory_space_constraint(values, pltpu.VMEM)


def in_hbm(values):
    return pltpu.with_memory_space_constraint(values, pltpu.HBM)


def body(t_upper, t_old, inverses, forcing, x_old, offsets, starts, column_map, z_cols, acc):
    n_col = lax.axis_size("col")
    n_row = lax.axis_size("row")
    row_idx = lax.axis_index("row")
    col_idx = lax.axis_index("col")
    steps, row_block, width = forcing.shape
    col_block = t_upper.shape[2]
    old_cols = x_old.shape[0]
    full_rows = col_block * n_col
    group = width // n_col
    share = row_block // n_col
    shape = jax.ShapeDtypeStruct

    def own_group(values):
        return lax.dynamic_slice_in_dim(values, col_idx * group, group, 0)

    gather = functools.partial(lax.all_gather, axis_name="col", axis=0)
    set_a = gather(inverses[2:3])

    old_base = steps * full_rows + col_idx * old_cols
    (old_part,) = pl.pallas_call(
        old_kernel,
        out_shape=[shape((n_col, group, steps * row_block), F32)],
        grid_spec=pltpu.PrefetchScalarGridSpec(
            num_scalar_prefetch=1,
            grid=(old_cols // CHUNK,),
            in_specs=[
                pl.BlockSpec((steps, row_block, CHUNK), lambda k, base: (0, 0, k)),
                pl.BlockSpec((CHUNK, width), lambda k, base: (k, 0)),
                pl.BlockSpec((1, width), lambda k, base: (0, 0)),
            ],
            out_specs=[
                pl.BlockSpec((n_col, group, steps * row_block), lambda k, base: (0, 0, 0))
            ],
            scratch_shapes=[pltpu.VMEM((width, steps * row_block), F32)],
        ),
        compiler_params=pltpu.CompilerParams(vmem_limit_bytes=VMEM_LIMIT),
        cost_estimate=pl.CostEstimate(
            flops=2 * t_old.size * width, bytes_accessed=2 * t_old.size, transcendentals=0
        ),
    )(old_base[None], in_hbm(t_old), in_hbm(x_old), starts[None, :])
    old_part, upper_later, inverses_later = lax.optimization_barrier(
        (old_part, t_upper, inverses)
    )
    old_part = lax.all_to_all(old_part, "col", 0, 0)
    set_b = gather(jnp.concatenate([upper_later[2:3], inverses_later[1:2]]))
    set_c = gather(jnp.concatenate([upper_later[:2], inverses_later[:1]]))
    inv = {2: (set_a, 0), 1: (set_b, 1), 0: (set_c, 2)}
    upper_of = {(1, 2): (set_b, 0), (0, 1): (set_c, 0), (0, 2): (set_c, 1)}

    core = col_idx % 2
    my_starts = own_group(starts)[:, None]
    my_offsets = own_group(offsets)[:, None]
    forcing_t = lax.dynamic_slice_in_dim(
        forcing.reshape(steps * row_block, width), col_idx * group, group, 1
    ).T
    limits = [my_starts - (step * full_rows + row_idx * row_block) for step in range(steps)]
    order = jnp.arange(2 * width, dtype=jnp.int32)
    half_of = order // group % 2
    value_of = order // (2 * group) * group + order % group
    target = jnp.concatenate([column_map, column_map + width])
    hot = ((half_of * width + value_of)[:, None] == target[None, :]).astype(BF16)
    old_part, my_offsets, forcing_t, limits, hot = lax.optimization_barrier(
        (old_part, my_offsets, forcing_t, limits, hot)
    )

    send_shape = shape((n_row, 2 * group, row_block), BF16)
    vec_shape = shape((group, row_block), F32)
    own_shape = shape((2 * group, row_block), BF16)
    flops = 4 * group * row_block * full_rows

    def spread(send):
        return lax.all_to_all(send, "row", 0, 0)

    rhs_all, send = call(
        functools.partial(first_kernel, steps - 1),
        [shape((group, steps * row_block), F32), send_shape],
        old_part,
        forcing_t,
    )
    whole = {}
    own = {}
    for step in reversed(range(steps)):
        if step < steps - 1:
            args = []
            uses = []
            for later in range(step + 1, steps):
                rows, which = upper_of[step, later]
                args += [whole[later], in_vmem(rows)]
                uses.append(which)
            (send,) = call(
                functools.partial(rhs_kernel, step, uses),
                [send_shape],
                *args,
                rhs_all,
                flops=flops * len(uses),
            )
        rows, which = inv[step]
        rows = in_vmem(rows)
        send, total = call(
            functools.partial(first_term_kernel, which),
            [send_shape, vec_shape],
            spread(send),
            rows,
            flops=flops,
        )
        for extra in range(1, NEUMANN):
            if extra < NEUMANN - 1:
                send, total = call(
                    functools.partial(next_term_kernel, which),
                    [send_shape, vec_shape],
                    spread(send),
                    rows,
                    my_offsets,
                    total,
                    flops=flops,
                )
            else:
                send, own[step] = call(
                    functools.partial(last_term_kernel, which),
                    [send_shape, own_shape],
                    spread(send),
                    rows,
                    my_offsets,
                    total,
                    limits[step],
                    flops=flops,
                )
        whole[step] = spread(send)

    early = list(range(1, steps))
    per = n_row // n_col
    z_rows = z_cols.shape[0]
    z_block = z_rows // n_col
    z_t = in_hbm(jnp.transpose(z_cols, (1, 0, 2)))
    z_params = pltpu.CompilerParams(vmem_limit_bytes=VMEM_LIMIT)

    def cost(parts):
        return pl.CostEstimate(
            flops=4 * z_rows * parts * col_block * width,
            bytes_accessed=2 * z_rows * parts * col_block,
            transcendentals=0,
        )

    gots = []
    mine = []
    for step in early:
        all_cols = gather(whole[step])
        gots.append(lax.dynamic_slice_in_dim(all_cols, per * col_idx, per, 1))
        rows = lax.dynamic_index_in_dim(all_cols, row_idx, 1, keepdims=False)
        mine.append(lax.dynamic_slice_in_dim(rows, col_idx * share, share, 2))
    (early_part,) = pl.pallas_call(
        z_early_kernel,
        out_shape=[shape((n_col, z_block, width), F32)],
        grid=(n_col,),
        in_specs=[pl.BlockSpec(got.shape, lambda i: (0, 0, 0, 0)) for got in gots]
        + [
            pl.BlockSpec(hot.shape, lambda i: (0, 0)),
            pl.BlockSpec((pl.Element(steps - 1), pl.Element(z_block), pl.Element(col_block)),
                         lambda i: (1, i * z_block, 0)),
        ],
        out_specs=[pl.BlockSpec((1, z_block, width), lambda i: (i, 0, 0))],
        scratch_shapes=[pltpu.VMEM((steps - 1, col_block, 2 * width), BF16)],
        compiler_params=z_params,
        cost_estimate=cost(steps - 1),
    )(*gots, hot, z_t)

    (send,) = call(
        columns_kernel,
        [shape((n_col, 2 * group, col_block + LANES), BF16)],
        whole[0],
        own[0],
    )
    got = lax.all_to_all(send, "col", 0, 0)

    last = lax.dynamic_slice_in_dim(
        got, col_block + col_idx % (LANES // share) * share, share, 2
    )
    mine = jnp.stack([last] + mine).astype(F32)
    mine = mine[:, :, :group] + mine[:, :, group:]
    solved = jnp.transpose(mine, (0, 3, 1, 2)).reshape(steps, share, width)

    def fixed(array_shape):
        return pl.BlockSpec(array_shape, lambda i, place: (0,) * len(array_shape))

    z_spec = pl.BlockSpec((1, z_block, col_block), lambda i, place: (0, 2 * i + place[0], 0))
    early_spec = pl.BlockSpec((1, z_block, width), lambda i, place: (2 * i + place[0], 0, 0))
    out_spec = pl.BlockSpec((1, z_block, width), lambda i, place: (i, 0, 0))
    part_shape = shape((n_col // 2, z_block, width), F32)
    picked_shape = shape((col_block, 2 * width), BF16)
    theirs, picked = pl.pallas_call(
        z_first_kernel,
        out_shape=[part_shape, picked_shape],
        grid_spec=pltpu.PrefetchScalarGridSpec(
            num_scalar_prefetch=1,
            grid=(n_col // 2,),
            in_specs=[fixed(got.shape), fixed(hot.shape), z_spec, early_spec],
            out_specs=[out_spec, fixed(picked_shape.shape)],
        ),
        compiler_params=z_params,
        cost_estimate=cost(1),
    )((1 - core)[None], got, hot, z_t, early_part)
    swapped = lax.ppermute(theirs, "col", [(i, i ^ 1) for i in range(n_col)])
    (ours,) = pl.pallas_call(
        z_next_kernel,
        out_shape=[part_shape],
        grid_spec=pltpu.PrefetchScalarGridSpec(
            num_scalar_prefetch=1,
            grid=(n_col // 2,),
            in_specs=[fixed(picked_shape.shape), z_spec, early_spec],
            out_specs=[out_spec],
        ),
        compiler_params=z_params,
        cost_estimate=cost(1),
    )(core[None], picked, z_t, early_part)
    part = lax.all_to_all(
        ours + swapped,
        "col",
        0,
        0,
        axis_index_groups=[list(range(c, n_col, 2)) for c in range(2)],
    )
    return (solved, acc + part.sum(0))


def solution(mesh):
    placed = (
        P(None, "row", "col"),
        P(None, "row", "col"),
        P(None, "row", "col"),
        P(None, "row", None),
        P("col", None),
        P(),
        P(),
        P(),
        P("row", None, "col"),
        P(("row", "col"), None),
    )
    return jax.shard_map(
        body,
        mesh=mesh,
        in_specs=placed,
        out_specs=(P(None, ("row", "col"), None), P(("row", "col"), None)),
        check_vma=False,
    )
```

```python
import functools

import jax
import jax.numpy as jnp
from jax import lax
from jax.experimental import pallas as pl
from jax.experimental.pallas import tpu as pltpu
from jax.sharding import PartitionSpec as P

NEUMANN = 3
F32 = jnp.float32
BF16 = jnp.bfloat16
VMEM_LIMIT = 16 << 20
LANES = 128
CHUNK = 768


def rows_product(pairs_ref, rows_ref, which):
    blocks, _, width = pairs_ref.shape
    per = blocks // rows_ref.shape[0]
    out = None
    for block in range(blocks):
        first = (block % per) * width
        part = lax.dot_general(
            pairs_ref[block],
            rows_ref[block // per, which, :, first : first + width],
            (((1,), (1,)), ((), ())),
            preferred_element_type=F32,
        )
        out = part if out is None else out + part
    half = out.shape[0] // 2
    return out[:half] + out[half:]


def pair_of(values):
    upper = values.astype(BF16)
    lower = (values - upper.astype(F32)).astype(BF16)
    return jnp.concatenate([upper, lower], axis=0)


def send_to_all(send_ref, pair):
    for peer in range(send_ref.shape[0]):
        send_ref[peer] = pair


def first_kernel(parts_ref, forcing_ref, send_ref):
    width = send_ref.shape[2]
    rhs = forcing_ref[:, -width:] - jnp.sum(parts_ref[...], axis=0)
    send_to_all(send_ref, pair_of(rhs))


def rhs_kernel(step, uses, *refs):
    forcing_ref, old_ref, send_ref = refs[-3:]
    width = send_ref.shape[2]
    here = slice(step * width, (step + 1) * width)
    rhs = forcing_ref[:, here] - old_ref[:, here]
    for k, which in enumerate(uses):
        rhs = rhs - rows_product(refs[2 * k], refs[2 * k + 1], which)
    send_to_all(send_ref, pair_of(rhs))


def load_kernel(from_ref, to_ref, sems):
    count = from_ref.shape[0]
    copies = [
        pltpu.make_async_copy(from_ref.at[k], to_ref.at[k], sems.at[k]) for k in range(count)
    ]
    for copy in copies:
        copy.start()
    for copy in copies:
        copy.wait()


def first_term_kernel(which, pairs_ref, rows_ref, send_ref, total_ref):
    term = rows_product(pairs_ref, rows_ref, which)
    total_ref[...] = term
    send_to_all(send_ref, pair_of(term))


def next_term_kernel(which, pairs_ref, rows_ref, scale_ref, old_ref, send_ref, total_ref):
    term = rows_product(pairs_ref, rows_ref, which) * scale_ref[...]
    total_ref[...] = old_ref[...] + term
    send_to_all(send_ref, pair_of(term))


def last_term_kernel(which, pairs_ref, rows_ref, scale_ref, old_ref, limit_ref, send_ref, own_ref):
    term = rows_product(pairs_ref, rows_ref, which) * scale_ref[...]
    total = old_ref[...] + term
    row = lax.broadcasted_iota(jnp.int32, total.shape, 1)
    pair = pair_of(jnp.where(row < limit_ref[...], total, 0.0))
    own_ref[...] = pair
    send_to_all(send_ref, pair)


def columns_kernel(whole_ref, own_ref, send_ref):
    n_col = send_ref.shape[0]
    blocks, _, width = whole_ref.shape
    per = blocks // n_col
    share = width // n_col
    for col in range(n_col):
        for k in range(per):
            send_ref[col, :, k * width : (k + 1) * width] = whole_ref[col * per + k]
        first = col * share // LANES * LANES
        send_ref[col, :, per * width :] = own_ref[:, first : first + LANES]


def pick(blocks, hot_ref):
    return lax.dot_general(
        jnp.concatenate(blocks, axis=0),
        hot_ref[...],
        (((0,), (0,)), ((), ())),
        preferred_element_type=F32,
    ).astype(BF16)


def fold(product):
    half = product.shape[1] // 2
    return product[:, :half] + product[:, half:]


def z_early_kernel(*refs):
    hot_ref, z_ref, out_ref, picked_ref = refs[-4:]
    gots = refs[:-4]

    @pl.when(pl.program_id(0) == 0)
    def _():
        for k, got_ref in enumerate(gots):
            per, cols, _, width = got_ref.shape
            for j in range(per):
                blocks = [got_ref[j, col] for col in range(cols)]
                picked_ref[k, j * width : (j + 1) * width] = pick(blocks, hot_ref)

    out = None
    for k in range(len(gots)):
        part = jnp.dot(z_ref[k], picked_ref[k], preferred_element_type=F32)
        out = part if out is None else out + part
    out_ref[0] = fold(out)


def z_first_kernel(place_ref, got_ref, hot_ref, z_ref, early_ref, out_ref, picked_ref):
    depth = z_ref.shape[2]

    @pl.when(pl.program_id(0) == 0)
    def _():
        blocks = [got_ref[k, :, :depth] for k in range(got_ref.shape[0])]
        picked_ref[...] = pick(blocks, hot_ref)

    z_next_kernel(place_ref, picked_ref, z_ref, early_ref, out_ref)


def z_next_kernel(place_ref, picked_ref, z_ref, early_ref, out_ref):
    product = jnp.dot(z_ref[0], picked_ref[...], preferred_element_type=F32)
    out_ref[0] = early_ref[0] + fold(product)


def old_kernel(base_ref, t_ref, old_ref, starts_ref, out_ref, rest_ref, sum_ref):
    k = pl.program_id(0)
    chunk = old_ref.shape[0]
    steps, rows, _ = t_ref.shape
    row = base_ref[0] + k * chunk + lax.broadcasted_iota(jnp.int32, old_ref.shape, 0)
    old = jnp.where(row < starts_ref[...], old_ref[...].astype(F32), 0.0).astype(BF16)
    for step in range(steps):
        part = jnp.dot(t_ref[step], old, preferred_element_type=F32)
        here = pl.ds(step * rows, rows)

        @pl.when(k == 0)
        def _():
            sum_ref[here] = part

        @pl.when(k > 0)
        def _():
            sum_ref[here] += part

    @pl.when(k == pl.num_programs(0) - 1)
    def _():
        group = out_ref.shape[1]
        last = sum_ref[(steps - 1) * rows :].T
        for col in range(out_ref.shape[0]):
            out_ref[col] = last[col * group : (col + 1) * group]
        rest_ref[...] = sum_ref[: (steps - 1) * rows].T


def call(kernel, outs, *args, flops=0):
    size = sum(a.size * a.dtype.itemsize for a in args)
    return pl.pallas_call(
        kernel,
        out_shape=outs,
        in_specs=[pl.BlockSpec(memory_space=pltpu.VMEM)] * len(args),
        out_specs=[pl.BlockSpec(memory_space=pltpu.VMEM)] * len(outs),
        compiler_params=pltpu.CompilerParams(vmem_limit_bytes=VMEM_LIMIT),
        cost_estimate=pl.CostEstimate(flops=flops, bytes_accessed=size, transcendentals=0),
    )(*args)


def in_vmem(values):
    return pltpu.with_memory_space_constraint(values, pltpu.VMEM)


def in_hbm(values):
    return pltpu.with_memory_space_constraint(values, pltpu.HBM)


def load(values):
    (out,) = pl.pallas_call(
        load_kernel,
        out_shape=[pltpu.VMEM(values.shape, values.dtype)],
        in_specs=[pl.BlockSpec(memory_space=pltpu.HBM)],
        out_specs=[pl.BlockSpec(memory_space=pltpu.VMEM)],
        scratch_shapes=[pltpu.SemaphoreType.DMA((values.shape[0],))],
        compiler_params=pltpu.CompilerParams(vmem_limit_bytes=VMEM_LIMIT),
        cost_estimate=pl.CostEstimate(
            flops=0, bytes_accessed=values.size * values.dtype.itemsize, transcendentals=0
        ),
    )(in_hbm(values))
    return out


def body(t_upper, t_old, inverses, forcing, x_old, offsets, starts, column_map, z_cols, acc):
    n_col = lax.axis_size("col")
    n_row = lax.axis_size("row")
    row_idx = lax.axis_index("row")
    col_idx = lax.axis_index("col")
    steps, row_block, width = forcing.shape
    col_block = t_upper.shape[2]
    old_cols = x_old.shape[0]
    full_rows = col_block * n_col
    group = width // n_col
    share = row_block // n_col
    shape = jax.ShapeDtypeStruct

    def own_group(values):
        return lax.dynamic_slice_in_dim(values, col_idx * group, group, 0)

    gather = functools.partial(lax.all_gather, axis_name="col", axis=0)
    gathered = {2: gather(inverses[2:3])}

    old_base = steps * full_rows + col_idx * old_cols
    old_part, old_rest = pl.pallas_call(
        old_kernel,
        out_shape=[
            shape((n_col, group, row_block), F32),
            shape((width, (steps - 1) * row_block), F32),
        ],
        grid_spec=pltpu.PrefetchScalarGridSpec(
            num_scalar_prefetch=1,
            grid=(old_cols // CHUNK,),
            in_specs=[
                pl.BlockSpec((steps, row_block, CHUNK), lambda k, base: (0, 0, k)),
                pl.BlockSpec((CHUNK, width), lambda k, base: (k, 0)),
                pl.BlockSpec((1, width), lambda k, base: (0, 0)),
            ],
            out_specs=[
                pl.BlockSpec((n_col, group, row_block), lambda k, base: (0, 0, 0)),
                pl.BlockSpec((width, (steps - 1) * row_block), lambda k, base: (0, 0)),
            ],
            scratch_shapes=[pltpu.VMEM((steps * row_block, width), F32)],
        ),
        compiler_params=pltpu.CompilerParams(vmem_limit_bytes=VMEM_LIMIT),
        cost_estimate=pl.CostEstimate(
            flops=2 * t_old.size * width, bytes_accessed=2 * t_old.size, transcendentals=0
        ),
    )(old_base[None], in_hbm(t_old), in_hbm(x_old), in_hbm(starts[None, :]))
    old_part = lax.all_to_all(old_part, "col", 0, 0)

    core = col_idx % 2
    my_starts = jnp.broadcast_to(own_group(starts)[:, None], (group, row_block))
    my_offsets = jnp.broadcast_to(own_group(offsets)[:, None], (group, row_block))
    forcing_t = lax.dynamic_slice_in_dim(
        forcing.reshape(steps * row_block, width), col_idx * group, group, 1
    ).T
    limits = [my_starts - (step * full_rows + row_idx * row_block) for step in range(steps)]
    order = jnp.arange(2 * width, dtype=jnp.int32)
    half_of = order // group % 2
    value_of = order // (2 * group) * group + order % group
    target = jnp.concatenate([column_map, column_map + width])
    hot = ((half_of * width + value_of)[:, None] == target[None, :]).astype(BF16)
    old_part, my_offsets, forcing_t, limits, hot, t_upper, inverses = lax.optimization_barrier(
        (old_part, my_offsets, forcing_t, limits, hot, t_upper, inverses)
    )
    gathered[1] = gather(jnp.concatenate([t_upper[2:3], inverses[1:2]]))
    which_inv = {2: 0, 1: 1, 0: 2}
    which_upper = {(1, 2): 0, (0, 1): 0, (0, 2): 1}

    send_shape = pltpu.VMEM((n_row, 2 * group, row_block), BF16)
    vec_shape = shape((group, row_block), F32)
    own_shape = shape((2 * group, row_block), BF16)
    flops = 4 * group * row_block * full_rows

    def spread(send):
        return lax.all_to_all(send, "row", 0, 0)

    (send,) = call(first_kernel, [send_shape], old_part, forcing_t)
    send, old_rest = lax.optimization_barrier((send, old_rest))
    old_rest = lax.psum_scatter(old_rest, "col", scatter_dimension=0, tiled=True)
    early = list(range(1, steps))
    per = n_row // n_col
    z_rows = z_cols.shape[0]
    z_block = z_rows // n_col
    z_t = in_hbm(jnp.transpose(z_cols, (1, 0, 2)))
    z_params = pltpu.CompilerParams(vmem_limit_bytes=VMEM_LIMIT)
    mine = []
    everywhere = {}

    def cost(parts):
        return pl.CostEstimate(
            flops=4 * z_rows * parts * col_block * width,
            bytes_accessed=2 * z_rows * parts * col_block,
            transcendentals=0,
        )

    def early_z():
        gots = []
        for step in early:
            blocks = everywhere[step].reshape(n_row, n_col, 2 * group, row_block)
            gots.append(lax.dynamic_slice_in_dim(blocks, per * col_idx, per, 0))
            rows = lax.dynamic_index_in_dim(blocks, row_idx, 0, keepdims=False)
            mine.append(lax.dynamic_slice_in_dim(rows, col_idx * share, share, 2))
        (out,) = pl.pallas_call(
            z_early_kernel,
            out_shape=[shape((n_col, z_block, width), F32)],
            grid=(n_col,),
            in_specs=[pl.BlockSpec(got.shape, lambda i: (0, 0, 0, 0)) for got in gots]
            + [
                pl.BlockSpec(hot.shape, lambda i: (0, 0)),
                pl.BlockSpec(
                    (pl.Element(steps - 1), pl.Element(z_block), pl.Element(col_block)),
                    lambda i: (1, i * z_block, 0),
                ),
            ],
            out_specs=[pl.BlockSpec((1, z_block, width), lambda i: (i, 0, 0))],
            scratch_shapes=[pltpu.VMEM((steps - 1, col_block, 2 * width), BF16)],
            compiler_params=z_params,
            cost_estimate=cost(steps - 1),
        )(*gots, hot, z_t)
        return out

    whole = {}
    own = {}
    for step in reversed(range(steps)):
        if step < steps - 1:
            got, rows, old_rest = lax.optimization_barrier(
                (whole[step + 1], gathered[step], old_rest)
            )
            rows = load(rows)
            whole[step + 1] = got
            args = []
            for later in range(step + 1, steps):
                args += [whole[later], rows]
            (send,) = call(
                functools.partial(
                    rhs_kernel, step, [which_upper[step, j] for j in range(step + 1, steps)]
                ),
                [send_shape],
                *args,
                forcing_t,
                old_rest,
                flops=flops * (steps - 1 - step),
            )
            got = spread(send)
        else:
            got, rows = lax.optimization_barrier((spread(send), gathered[step]))
            rows = load(rows)
        which = which_inv[step]
        send, total = call(
            functools.partial(first_term_kernel, which),
            [send_shape, vec_shape],
            got,
            rows,
            flops=flops,
        )
        if step == steps - 1:
            send, t_upper, inverses = lax.optimization_barrier((send, t_upper, inverses))
            gathered[0] = gather(jnp.concatenate([t_upper[:2], inverses[:1]]))
        for extra in range(1, NEUMANN - 1):
            send, total = call(
                functools.partial(next_term_kernel, which),
                [send_shape, vec_shape],
                spread(send),
                rows,
                my_offsets,
                total,
                flops=flops,
            )
        send, own[step] = call(
            functools.partial(last_term_kernel, which),
            [send_shape, own_shape],
            spread(send),
            rows,
            my_offsets,
            total,
            limits[step],
            flops=flops,
        )
        if step > 0:
            everywhere[step] = lax.all_gather(own[step], ("row", "col"), axis=0)
        else:
            own[0], everywhere = lax.optimization_barrier((own[0], everywhere))
        whole[step] = spread(send)
    whole[0], early_part = lax.optimization_barrier((whole[0], early_z()))

    (send,) = call(
        columns_kernel,
        [shape((n_col, 2 * group, col_block + LANES), BF16)],
        whole[0],
        own[0],
    )
    got = lax.all_to_all(send, "col", 0, 0)

    last = lax.dynamic_slice_in_dim(
        got, col_block + col_idx % (LANES // share) * share, share, 2
    )
    mine = jnp.stack([last] + mine).astype(F32)
    mine = mine[:, :, :group] + mine[:, :, group:]
    solved = jnp.transpose(mine, (0, 3, 1, 2)).reshape(steps, share, width)

    def fixed(array_shape):
        return pl.BlockSpec(array_shape, lambda i, place: (0,) * len(array_shape))

    z_spec = pl.BlockSpec((1, z_block, col_block), lambda i, place: (0, 2 * i + place[0], 0))
    early_spec = pl.BlockSpec((1, z_block, width), lambda i, place: (2 * i + place[0], 0, 0))
    out_spec = pl.BlockSpec((1, z_block, width), lambda i, place: (i, 0, 0))
    part_shape = pltpu.VMEM((n_col // 2, z_block, width), F32)
    picked_shape = shape((col_block, 2 * width), BF16)
    theirs, picked = pl.pallas_call(
        z_first_kernel,
        out_shape=[part_shape, picked_shape],
        grid_spec=pltpu.PrefetchScalarGridSpec(
            num_scalar_prefetch=1,
            grid=(n_col // 2,),
            in_specs=[fixed(got.shape), fixed(hot.shape), z_spec, early_spec],
            out_specs=[out_spec, fixed(picked_shape.shape)],
        ),
        compiler_params=z_params,
        cost_estimate=cost(1),
    )((1 - core)[None], got, hot, z_t, early_part)
    swapped = lax.ppermute(theirs, "col", [(i, i ^ 1) for i in range(n_col)])
    (ours,) = pl.pallas_call(
        z_next_kernel,
        out_shape=[part_shape],
        grid_spec=pltpu.PrefetchScalarGridSpec(
            num_scalar_prefetch=1,
            grid=(n_col // 2,),
            in_specs=[fixed(picked_shape.shape), z_spec, early_spec],
            out_specs=[out_spec],
        ),
        compiler_params=z_params,
        cost_estimate=cost(1),
    )(core[None], picked, z_t, early_part)
    part = lax.all_to_all(
        ours + swapped,
        "col",
        0,
        0,
        axis_index_groups=[list(range(c, n_col, 2)) for c in range(2)],
    )
    return (solved, acc + part.sum(0))


def solution(mesh):
    placed = (
        P(None, "row", "col"),
        P(None, "row", "col"),
        P(None, "row", "col"),
        P(None, "row", None),
        P("col", None),
        P(),
        P(),
        P(),
        P("row", None, "col"),
        P(("row", "col"), None),
    )
    return jax.shard_map(
        body,
        mesh=mesh,
        in_specs=placed,
        out_specs=(P(None, ("row", "col"), None), P(("row", "col"), None)),
        check_vma=False,
    )
```

```python
import functools

import jax
import jax.numpy as jnp
from jax import lax
from jax.experimental import pallas as pl
from jax.experimental.pallas import tpu as pltpu
from jax.sharding import PartitionSpec as P

NEUMANN = 3
F32 = jnp.float32
BF16 = jnp.bfloat16
VMEM_LIMIT = 16 << 20
LANES = 128
CHUNK = 768


def rows_product(pairs_ref, rows_ref, which):
    blocks, _, width = pairs_ref.shape
    per = blocks // rows_ref.shape[0]
    out = None
    for block in range(blocks):
        first = (block % per) * width
        part = lax.dot_general(
            pairs_ref[block],
            rows_ref[block // per, which, :, first : first + width],
            (((1,), (1,)), ((), ())),
            preferred_element_type=F32,
        )
        out = part if out is None else out + part
    half = out.shape[0] // 2
    return out[:half] + out[half:]


def pair_of(values):
    upper = values.astype(BF16)
    lower = (values - upper.astype(F32)).astype(BF16)
    return jnp.concatenate([upper, lower], axis=0)


def send_to_all(send_ref, pair):
    for peer in range(send_ref.shape[0]):
        send_ref[peer] = pair


def first_kernel(parts_ref, forcing_ref, rest_ref, send_ref):
    width = send_ref.shape[2]
    rhs = forcing_ref[...] - jnp.sum(parts_ref[...], axis=0)
    rest_ref[...] = rhs[:, :-width]
    send_to_all(send_ref, pair_of(rhs[:, -width:]))


def rhs_kernel(step, uses, *refs):
    rhs_ref, send_ref = refs[-2:]
    width = send_ref.shape[2]
    rhs = rhs_ref[:, step * width : (step + 1) * width]
    for k, which in enumerate(uses):
        rhs = rhs - rows_product(refs[2 * k], refs[2 * k + 1], which)
    send_to_all(send_ref, pair_of(rhs))


def load_kernel(from_ref, to_ref, sems):
    count = from_ref.shape[0]
    copies = [
        pltpu.make_async_copy(from_ref.at[k], to_ref.at[k], sems.at[k]) for k in range(count)
    ]
    for copy in copies:
        copy.start()
    for copy in copies:
        copy.wait()


def first_term_kernel(which, pairs_ref, rows_ref, send_ref, total_ref):
    term = rows_product(pairs_ref, rows_ref, which)
    total_ref[...] = term
    send_to_all(send_ref, pair_of(term))


def next_term_kernel(which, pairs_ref, rows_ref, scale_ref, old_ref, send_ref, total_ref):
    term = rows_product(pairs_ref, rows_ref, which) * scale_ref[...]
    total_ref[...] = old_ref[...] + term
    send_to_all(send_ref, pair_of(term))


def last_term_kernel(which, pairs_ref, rows_ref, scale_ref, old_ref, limit_ref, send_ref, own_ref):
    term = rows_product(pairs_ref, rows_ref, which) * scale_ref[...]
    total = old_ref[...] + term
    row = lax.broadcasted_iota(jnp.int32, total.shape, 1)
    pair = pair_of(jnp.where(row < limit_ref[...], total, 0.0))
    own_ref[...] = pair
    send_to_all(send_ref, pair)


def last_streamed_kernel(
    which, pairs_ref, rows_ref, scale_ref, old_ref, limit_ref, send_ref, own_ref, tiles_ref, sems
):
    copies = [
        pltpu.make_async_copy(rows_ref.at[k, which], tiles_ref.at[k, 0], sems.at[k])
        for k in range(rows_ref.shape[0])
    ]
    for copy in copies:
        copy.start()
    for copy in copies:
        copy.wait()
    last_term_kernel(
        0, pairs_ref, tiles_ref, scale_ref, old_ref, limit_ref, send_ref, own_ref
    )


def columns_kernel(whole_ref, own_ref, send_ref):
    n_col = send_ref.shape[0]
    blocks, _, width = whole_ref.shape
    per = blocks // n_col
    share = width // n_col
    for col in range(n_col):
        for k in range(per):
            send_ref[col, :, k * width : (k + 1) * width] = whole_ref[col * per + k]
        first = col * share // LANES * LANES
        send_ref[col, :, per * width :] = own_ref[:, first : first + LANES]


def pick(blocks, hot_ref):
    return lax.dot_general(
        jnp.concatenate(blocks, axis=0),
        hot_ref[...],
        (((0,), (0,)), ((), ())),
        preferred_element_type=F32,
    ).astype(BF16)


def fold(product):
    half = product.shape[1] // 2
    return product[:, :half] + product[:, half:]


def z_early_kernel(place_ref, *refs):
    hot_ref, z_ref, out_ref, picked_ref = refs[-4:]
    gots = refs[:-4]

    @pl.when(pl.program_id(0) == 0)
    def _():
        for k, got_ref in enumerate(gots):
            cols, per, _, width = got_ref.shape
            for j in range(per):
                blocks = [got_ref[col, j] for col in range(cols)]
                picked_ref[k, j * width : (j + 1) * width] = pick(blocks, hot_ref)

    out = None
    for k in range(len(gots)):
        part = jnp.dot(z_ref[k], picked_ref[k], preferred_element_type=F32)
        out = part if out is None else out + part
    out_ref[...] = fold(out).reshape(out_ref.shape)


def z_tiles(place_ref, z_ref, early_ref, tiles_ref, adds_ref, sems):
    copies = []
    count, size, _ = tiles_ref.shape
    for k in range(count):
        block = 2 * k + place_ref[0]
        rows = pl.ds(pl.multiple_of(block * size, size), size)
        copies.append(
            (
                pltpu.make_async_copy(z_ref.at[0, rows], tiles_ref.at[k], sems.at[0, k]),
                pltpu.make_async_copy(early_ref.at[block], adds_ref.at[k], sems.at[1, k]),
            )
        )
        for copy in copies[-1]:
            copy.start()
    return copies


def z_products(copies, picked, tiles_ref, adds_ref, out_ref):
    for k, both in enumerate(copies):
        for copy in both:
            copy.wait()
        product = jnp.dot(tiles_ref[k], picked, preferred_element_type=F32)
        out_ref[k] = adds_ref[k] + fold(product)


def z_first_kernel(
    place_ref, got_ref, hot_ref, z_ref, early_ref, out_ref, picked_ref, tiles_ref, adds_ref, sems
):
    copies = z_tiles(place_ref, z_ref, early_ref, tiles_ref, adds_ref, sems)
    depth = z_ref.shape[2]
    picked_ref[...] = pick([got_ref[k, :, :depth] for k in range(got_ref.shape[0])], hot_ref)
    z_products(copies, picked_ref[...], tiles_ref, adds_ref, out_ref)


def z_next_kernel(place_ref, picked_ref, z_ref, early_ref, out_ref, tiles_ref, adds_ref, sems):
    copies = z_tiles(place_ref, z_ref, early_ref, tiles_ref, adds_ref, sems)
    z_products(copies, picked_ref[...], tiles_ref, adds_ref, out_ref)


def old_kernel(base_ref, t_ref, old_ref, starts_ref, out_ref, sum_ref):
    k = pl.program_id(0)
    chunk = old_ref.shape[0]
    steps, rows, _ = t_ref.shape
    row = base_ref[0] + k * chunk + lax.broadcasted_iota(jnp.int32, old_ref.shape, 0)
    old = jnp.where(row < starts_ref[...], old_ref[...].astype(F32), 0.0).astype(BF16)
    t = t_ref[...].reshape(steps * rows, chunk)
    part = jnp.dot(t, old, preferred_element_type=F32)

    @pl.when(k == 0)
    def _():
        sum_ref[...] = part

    @pl.when(k > 0)
    def _():
        sum_ref[...] += part

    @pl.when(k == pl.num_programs(0) - 1)
    def _():
        group = out_ref.shape[1]
        whole = sum_ref[...].T
        for col in range(out_ref.shape[0]):
            out_ref[col] = whole[col * group : (col + 1) * group]


def call(kernel, outs, *args, flops=0):
    size = sum(a.size * a.dtype.itemsize for a in args)
    return pl.pallas_call(
        kernel,
        out_shape=outs,
        in_specs=[pl.BlockSpec(memory_space=pltpu.VMEM)] * len(args),
        out_specs=[pl.BlockSpec(memory_space=pltpu.VMEM)] * len(outs),
        compiler_params=pltpu.CompilerParams(vmem_limit_bytes=VMEM_LIMIT),
        cost_estimate=pl.CostEstimate(flops=flops, bytes_accessed=size, transcendentals=0),
    )(*args)


def in_vmem(values):
    return pltpu.with_memory_space_constraint(values, pltpu.VMEM)


def in_hbm(values):
    return pltpu.with_memory_space_constraint(values, pltpu.HBM)


def load(values):
    (out,) = pl.pallas_call(
        load_kernel,
        out_shape=[pltpu.VMEM(values.shape, values.dtype)],
        in_specs=[pl.BlockSpec(memory_space=pltpu.HBM)],
        out_specs=[pl.BlockSpec(memory_space=pltpu.VMEM)],
        scratch_shapes=[pltpu.SemaphoreType.DMA((values.shape[0],))],
        compiler_params=pltpu.CompilerParams(vmem_limit_bytes=VMEM_LIMIT),
        cost_estimate=pl.CostEstimate(
            flops=0, bytes_accessed=values.size * values.dtype.itemsize, transcendentals=0
        ),
    )(in_hbm(values))
    return out


def body(t_upper, t_old, inverses, forcing, x_old, offsets, starts, column_map, z_cols, acc):
    n_col = lax.axis_size("col")
    n_row = lax.axis_size("row")
    row_idx = lax.axis_index("row")
    col_idx = lax.axis_index("col")
    steps, row_block, width = forcing.shape
    col_block = t_upper.shape[2]
    old_cols = x_old.shape[0]
    full_rows = col_block * n_col
    group = width // n_col
    share = row_block // n_col
    shape = jax.ShapeDtypeStruct

    def own_group(values):
        return lax.dynamic_slice_in_dim(values, col_idx * group, group, 0)

    gather = functools.partial(lax.all_gather, axis_name="col", axis=0)
    gathered = {2: gather(inverses[2:3])}

    old_base = steps * full_rows + col_idx * old_cols
    (old_part,) = pl.pallas_call(
        old_kernel,
        out_shape=[
            shape((n_col, group, steps * row_block), F32),
        ],
        grid_spec=pltpu.PrefetchScalarGridSpec(
            num_scalar_prefetch=1,
            grid=(old_cols // CHUNK,),
            in_specs=[
                pl.BlockSpec((steps, row_block, CHUNK), lambda k, base: (0, 0, k)),
                pl.BlockSpec((CHUNK, width), lambda k, base: (k, 0)),
                pl.BlockSpec((1, width), lambda k, base: (0, 0)),
            ],
            out_specs=[
                pl.BlockSpec((n_col, group, steps * row_block), lambda k, base: (0, 0, 0)),
            ],
            scratch_shapes=[pltpu.VMEM((steps * row_block, width), F32)],
        ),
        compiler_params=pltpu.CompilerParams(vmem_limit_bytes=VMEM_LIMIT),
        cost_estimate=pl.CostEstimate(
            flops=2 * t_old.size * width, bytes_accessed=2 * t_old.size, transcendentals=0
        ),
    )(old_base[None], in_hbm(t_old), in_hbm(x_old), in_hbm(starts[None, :]))
    old_part = lax.all_to_all(old_part, "col", 0, 0)

    core = col_idx % 2
    my_starts = jnp.broadcast_to(own_group(starts)[:, None], (group, row_block))
    my_offsets = jnp.broadcast_to(own_group(offsets)[:, None], (group, row_block))
    forcing_t = lax.dynamic_slice_in_dim(
        forcing.reshape(steps * row_block, width), col_idx * group, group, 1
    ).T
    limits = [my_starts - (step * full_rows + row_idx * row_block) for step in range(steps)]
    order = jnp.arange(2 * width, dtype=jnp.int32)
    half_of = order // group % 2
    value_of = order // (2 * group) * group + order % group
    target = jnp.concatenate([column_map, column_map + width])
    hot = ((half_of * width + value_of)[:, None] == target[None, :]).astype(BF16)
    old_part, my_offsets, forcing_t, limits, hot, t_upper, inverses = lax.optimization_barrier(
        (old_part, my_offsets, forcing_t, limits, hot, t_upper, inverses)
    )
    gathered[1] = gather(jnp.concatenate([t_upper[2:3], inverses[1:2]]))
    which_inv = {2: 0, 1: 1, 0: 2}
    which_upper = {(1, 2): 0, (0, 1): 0, (0, 2): 1}

    send_shape = pltpu.VMEM((n_row, 2 * group, row_block), BF16)
    vec_shape = shape((group, row_block), F32)
    own_shape = shape((2 * group, row_block), BF16)
    flops = 4 * group * row_block * full_rows

    def spread(send):
        return lax.all_to_all(send, "row", 0, 0)

    rest_shape = shape((group, (steps - 1) * row_block), F32)
    rhs_rest, send = call(first_kernel, [rest_shape, send_shape], old_part, forcing_t)
    early = list(range(1, steps))
    per = n_row // n_col
    z_rows = z_cols.shape[0]
    z_block = z_rows // n_col
    z_t = in_hbm(jnp.transpose(z_cols, (1, 0, 2)))
    z_params = pltpu.CompilerParams(vmem_limit_bytes=VMEM_LIMIT)
    mine = []
    everywhere = {}

    def cost(parts):
        return pl.CostEstimate(
            flops=4 * z_rows * parts * col_block * width,
            bytes_accessed=2 * z_rows * parts * col_block,
            transcendentals=0,
        )

    def early_z():
        gots = []
        for step in early:
            blocks = everywhere[step]
            gots.append(blocks)
            rows = lax.dynamic_index_in_dim(blocks, row_idx, 1, keepdims=False)
            mine.append(lax.dynamic_slice_in_dim(rows, col_idx * share, share, 2))
        tile = 2
        (out,) = pl.pallas_call(
            z_early_kernel,
            out_shape=[pltpu.HBM((n_col, z_block, width), F32)],
            grid_spec=pltpu.PrefetchScalarGridSpec(
                num_scalar_prefetch=1,
                grid=(n_col // tile,),
                in_specs=[
                    pl.BlockSpec(
                        (n_col, per, 2 * group, row_block), lambda i, place: (0, place[0], 0, 0)
                    )
                    for _ in gots
                ]
                + [
                    pl.BlockSpec(hot.shape, lambda i, place: (0, 0)),
                    pl.BlockSpec(
                        (pl.Element(steps - 1), pl.Element(tile * z_block), pl.Element(col_block)),
                        lambda i, place: (1, i * (tile * z_block), 0),
                    ),
                ],
                out_specs=[pl.BlockSpec((tile, z_block, width), lambda i, place: (i, 0, 0))],
                scratch_shapes=[pltpu.VMEM((steps - 1, col_block, 2 * width), BF16)],
            ),
            compiler_params=z_params,
            cost_estimate=cost(steps - 1),
        )(col_idx[None], *[in_hbm(got) for got in gots], hot, z_t)
        return out

    whole = {}
    own = {}
    for step in reversed(range(steps)):
        if step < steps - 1:
            got, rows = lax.optimization_barrier((whole[step + 1], gathered[step]))
            rows = load(rows)
            whole[step + 1] = got
            args = []
            for later in range(step + 1, steps):
                args += [whole[later], rows]
            (send,) = call(
                functools.partial(
                    rhs_kernel, step, [which_upper[step, j] for j in range(step + 1, steps)]
                ),
                [send_shape],
                *args,
                rhs_rest,
                flops=flops * (steps - 1 - step),
            )
            got = spread(send)
        else:
            got, rows = lax.optimization_barrier((spread(send), gathered[step]))
            rows = load(rows)
        which = which_inv[step]
        send, total = call(
            functools.partial(first_term_kernel, which),
            [send_shape, vec_shape],
            got,
            rows,
            flops=flops,
        )
        if step == steps - 1:
            send, t_upper, inverses = lax.optimization_barrier((send, t_upper, inverses))
            gathered[0] = gather(jnp.concatenate([t_upper[:2], inverses[:1]]))
        for extra in range(1, NEUMANN - 1):
            send, total = call(
                functools.partial(next_term_kernel, which),
                [send_shape, vec_shape],
                spread(send),
                rows,
                my_offsets,
                total,
                flops=flops,
            )
        if step > 0:
            send, own[step] = call(
                functools.partial(last_term_kernel, which),
                [send_shape, own_shape],
                spread(send),
                rows,
                my_offsets,
                total,
                limits[step],
                flops=flops,
            )
        else:
            vm = pl.BlockSpec(memory_space=pltpu.VMEM)
            rows = gathered[0]
            send, own[0] = pl.pallas_call(
                functools.partial(last_streamed_kernel, which),
                out_shape=[send_shape, own_shape],
                in_specs=[vm, pl.BlockSpec(memory_space=pltpu.HBM), vm, vm, vm],
                out_specs=[vm, vm],
                scratch_shapes=[
                    pltpu.VMEM((n_col, 1, row_block, col_block), BF16),
                    pltpu.SemaphoreType.DMA((n_col,)),
                ],
                compiler_params=pltpu.CompilerParams(vmem_limit_bytes=VMEM_LIMIT),
                cost_estimate=pl.CostEstimate(
                    flops=flops, bytes_accessed=2 * row_block * full_rows, transcendentals=0
                ),
            )(spread(send), in_hbm(rows), my_offsets, total, limits[0])
        if step == 0:
            own[0], everywhere = lax.optimization_barrier((own[0], everywhere))
        whole[step] = spread(send)
        if step > 0:
            everywhere[step] = gather(whole[step])
    whole[0], early_part = lax.optimization_barrier((whole[0], early_z()))

    (send,) = call(
        columns_kernel,
        [shape((n_col, 2 * group, col_block + LANES), BF16)],
        whole[0],
        own[0],
    )
    got = lax.all_to_all(send, "col", 0, 0)

    last = lax.dynamic_slice_in_dim(
        got, col_block + col_idx % (LANES // share) * share, share, 2
    )
    mine = jnp.stack([last] + mine).astype(F32)
    mine = mine[:, :, :group] + mine[:, :, group:]
    solved = jnp.transpose(mine, (0, 3, 1, 2)).reshape(steps, share, width)

    part_shape = shape((n_col // 2, z_block, width), F32)
    picked_shape = shape((col_block, 2 * width), BF16)
    in_vm = pl.BlockSpec(memory_space=pltpu.VMEM)
    in_hb = pl.BlockSpec(memory_space=pltpu.HBM)
    scalar = pl.BlockSpec(memory_space=pltpu.SMEM)
    scratch = [
        pltpu.VMEM((n_col // 2, z_block, col_block), BF16),
        pltpu.VMEM((n_col // 2, z_block, width), F32),
        pltpu.SemaphoreType.DMA((2, n_col // 2)),
    ]
    early_part = in_hbm(early_part)
    theirs, picked = pl.pallas_call(
        z_first_kernel,
        out_shape=[part_shape, picked_shape],
        in_specs=[scalar, in_vm, in_vm, in_hb, in_hb],
        out_specs=[in_vm, in_vm],
        scratch_shapes=scratch,
        compiler_params=z_params,
        cost_estimate=cost(1),
    )((1 - core)[None], got, hot, z_t, early_part)
    swapped = lax.ppermute(theirs, "col", [(i, i ^ 1) for i in range(n_col)])
    (ours,) = pl.pallas_call(
        z_next_kernel,
        out_shape=[part_shape],
        in_specs=[scalar, in_vm, in_hb, in_hb],
        out_specs=[in_vm],
        scratch_shapes=scratch,
        compiler_params=z_params,
        cost_estimate=cost(1),
    )(core[None], picked, z_t, early_part)
    part = lax.all_to_all(
        ours + swapped,
        "col",
        0,
        0,
        axis_index_groups=[list(range(c, n_col, 2)) for c in range(2)],
    )
    return (solved, acc + part.sum(0))


def solution(mesh):
    placed = (
        P(None, "row", "col"),
        P(None, "row", "col"),
        P(None, "row", "col"),
        P(None, "row", None),
        P("col", None),
        P(),
        P(),
        P(),
        P("row", None, "col"),
        P(("row", "col"), None),
    )
    return jax.shard_map(
        body,
        mesh=mesh,
        in_specs=placed,
        out_specs=(P(None, ("row", "col"), None), P(("row", "col"), None)),
        check_vma=False,
    )
```

```python
import functools

import jax
import jax.numpy as jnp
from jax import lax
from jax.experimental import pallas as pl
from jax.experimental.pallas import tpu as pltpu
from jax.sharding import PartitionSpec as P

NEUMANN = 3
F32 = jnp.float32
BF16 = jnp.bfloat16
VMEM_LIMIT = 16 << 20
LANES = 128
CHUNK = 768


def rows_product(pairs_ref, rows_ref, which, copies=None):
    blocks, _, width = pairs_ref.shape
    per = blocks // rows_ref.shape[0]
    out = None
    for block in range(blocks):
        first = (block % per) * width
        if copies is not None and first == 0:
            copies[block // per].wait()
        part = lax.dot_general(
            pairs_ref[block],
            rows_ref[block // per, which, :, first : first + width],
            (((1,), (1,)), ((), ())),
            preferred_element_type=F32,
        )
        out = part if out is None else out + part
    half = out.shape[0] // 2
    return out[:half] + out[half:]


def pair_of(values):
    upper = values.astype(BF16)
    lower = (values - upper.astype(F32)).astype(BF16)
    return jnp.concatenate([upper, lower], axis=0)


def send_to_all(send_ref, pair):
    for peer in range(send_ref.shape[0]):
        send_ref[peer] = pair


def first_kernel(parts_ref, forcing_ref, rest_ref, send_ref):
    width = send_ref.shape[2]
    rhs = forcing_ref[...] - jnp.sum(parts_ref[...], axis=0)
    rest_ref[...] = rhs[:, :-width]
    send_to_all(send_ref, pair_of(rhs[:, -width:]))


def stream(rows_ref, uses, tiles_ref, sems):
    copies = []
    for k, which in enumerate(uses):
        copies.append(
            [
                pltpu.make_async_copy(rows_ref.at[j, which], tiles_ref.at[j, k], sems.at[j, k])
                for j in range(rows_ref.shape[0])
            ]
        )
        for copy in copies[-1]:
            copy.start()
    return copies


def rhs_kernel(step, uses, *refs):
    rows_ref, rhs_ref, send_ref, tiles_ref, sems, pairs_ref, pair_sems = refs[-7:]
    count = len(uses)
    firsts = [
        pltpu.make_async_copy(refs[k], pairs_ref.at[k], pair_sems.at[k]) for k in range(count)
    ]
    for copy in firsts:
        copy.start()
    copies = stream(rows_ref, uses, tiles_ref, sems)
    width = send_ref.shape[2]
    rhs = rhs_ref[:, step * width : (step + 1) * width]
    for k in range(count):
        firsts[k].wait()
        rhs = rhs - rows_product(pairs_ref.at[k], tiles_ref, k, copies[k])
    send_to_all(send_ref, pair_of(rhs))


def first_streamed_kernel(which, pairs_ref, rows_ref, send_ref, total_ref, tiles_ref, sems):
    copies = stream(rows_ref, [which], tiles_ref, sems)
    term = rows_product(pairs_ref, tiles_ref, 0, copies[0])
    total_ref[...] = term
    send_to_all(send_ref, pair_of(term))


def first_term_kernel(which, pairs_ref, rows_ref, send_ref, total_ref):
    term = rows_product(pairs_ref, rows_ref, which)
    total_ref[...] = term
    send_to_all(send_ref, pair_of(term))


def next_term_kernel(which, pairs_ref, rows_ref, scale_ref, old_ref, send_ref, total_ref):
    term = rows_product(pairs_ref, rows_ref, which) * scale_ref[...]
    total_ref[...] = old_ref[...] + term
    send_to_all(send_ref, pair_of(term))


def last_term_kernel(which, pairs_ref, rows_ref, scale_ref, old_ref, limit_ref, send_ref, own_ref):
    term = rows_product(pairs_ref, rows_ref, which) * scale_ref[...]
    total = old_ref[...] + term
    row = lax.broadcasted_iota(jnp.int32, total.shape, 1)
    pair = pair_of(jnp.where(row < limit_ref[...], total, 0.0))
    own_ref[...] = pair
    send_to_all(send_ref, pair)


def columns_kernel(whole_ref, own_ref, send_ref):
    n_col = send_ref.shape[0]
    blocks, _, width = whole_ref.shape
    per = blocks // n_col
    share = width // n_col
    for col in range(n_col):
        for k in range(per):
            send_ref[col, :, k * width : (k + 1) * width] = whole_ref[col * per + k]
        first = col * share // LANES * LANES
        send_ref[col, :, per * width :] = own_ref[:, first : first + LANES]


def pick(blocks, hot_ref):
    return lax.dot_general(
        jnp.concatenate(blocks, axis=0),
        hot_ref[...],
        (((0,), (0,)), ((), ())),
        preferred_element_type=F32,
    ).astype(BF16)


def fold(product):
    half = product.shape[1] // 2
    return product[:, :half] + product[:, half:]


def z_early_kernel(place_ref, *refs):
    hot_ref, z_ref, out_ref, picked_ref = refs[-4:]
    gots = refs[:-4]

    @pl.when(pl.program_id(0) == 0)
    def _():
        for k, got_ref in enumerate(gots):
            cols, per, _, width = got_ref.shape
            for j in range(per):
                blocks = [got_ref[col, j] for col in range(cols)]
                picked_ref[k, j * width : (j + 1) * width] = pick(blocks, hot_ref)

    out = None
    for k in range(len(gots)):
        part = jnp.dot(z_ref[k], picked_ref[k], preferred_element_type=F32)
        out = part if out is None else out + part
    out_ref[...] = fold(out).reshape(out_ref.shape)


def z_tiles(place_ref, z_ref, early_ref, tiles_ref, adds_ref, sems):
    copies = []
    count, size, _ = tiles_ref.shape
    for k in range(count):
        block = 2 * k + place_ref[0]
        rows = pl.ds(pl.multiple_of(block * size, size), size)
        copies.append(
            (
                pltpu.make_async_copy(z_ref.at[0, rows], tiles_ref.at[k], sems.at[0, k]),
                pltpu.make_async_copy(early_ref.at[block], adds_ref.at[k], sems.at[1, k]),
            )
        )
        for copy in copies[-1]:
            copy.start()
    return copies


def z_products(copies, picked, tiles_ref, adds_ref, out_ref):
    for k, both in enumerate(copies):
        for copy in both:
            copy.wait()
        product = jnp.dot(tiles_ref[k], picked, preferred_element_type=F32)
        out_ref[k] = adds_ref[k] + fold(product)


def z_first_kernel(
    place_ref, got_ref, hot_ref, z_ref, early_ref, out_ref, picked_ref, tiles_ref, adds_ref, sems
):
    copies = z_tiles(place_ref, z_ref, early_ref, tiles_ref, adds_ref, sems)
    depth = z_ref.shape[2]
    picked_ref[...] = pick([got_ref[k, :, :depth] for k in range(got_ref.shape[0])], hot_ref)
    z_products(copies, picked_ref[...], tiles_ref, adds_ref, out_ref)


def z_next_kernel(place_ref, picked_ref, z_ref, early_ref, out_ref, tiles_ref, adds_ref, sems):
    copies = z_tiles(place_ref, z_ref, early_ref, tiles_ref, adds_ref, sems)
    z_products(copies, picked_ref[...], tiles_ref, adds_ref, out_ref)


def old_kernel(base_ref, t_ref, old_ref, starts_ref, out_ref, sum_ref):
    k = pl.program_id(0)
    chunk = old_ref.shape[0]
    steps, rows, _ = t_ref.shape
    row = base_ref[0] + k * chunk + lax.broadcasted_iota(jnp.int32, old_ref.shape, 0)
    old = jnp.where(row < starts_ref[...], old_ref[...].astype(F32), 0.0).astype(BF16)
    t = t_ref[...].reshape(steps * rows, chunk)
    part = jnp.dot(t, old, preferred_element_type=F32)

    @pl.when(k == 0)
    def _():
        sum_ref[...] = part

    @pl.when(k > 0)
    def _():
        sum_ref[...] += part

    @pl.when(k == pl.num_programs(0) - 1)
    def _():
        group = out_ref.shape[1]
        whole = sum_ref[...].T
        for col in range(out_ref.shape[0]):
            out_ref[col] = whole[col * group : (col + 1) * group]


def call(kernel, outs, *args, flops=0):
    size = sum(a.size * a.dtype.itemsize for a in args)
    return pl.pallas_call(
        kernel,
        out_shape=outs,
        in_specs=[pl.BlockSpec(memory_space=pltpu.VMEM)] * len(args),
        out_specs=[pl.BlockSpec(memory_space=pltpu.VMEM)] * len(outs),
        compiler_params=pltpu.CompilerParams(vmem_limit_bytes=VMEM_LIMIT),
        cost_estimate=pl.CostEstimate(flops=flops, bytes_accessed=size, transcendentals=0),
    )(*args)


def in_vmem(values):
    return pltpu.with_memory_space_constraint(values, pltpu.VMEM)


def in_hbm(values):
    return pltpu.with_memory_space_constraint(values, pltpu.HBM)


def call_streamed(kernel, uses, outs, vectors, rows, rest=(), stream_vectors=False, flops=0):
    vm = pl.BlockSpec(memory_space=pltpu.VMEM)
    hb = pl.BlockSpec(memory_space=pltpu.HBM)
    cols, _, height, width = rows.shape
    scratch = [
        pltpu.VMEM((cols, len(uses), height, width), rows.dtype),
        pltpu.SemaphoreType.DMA((cols, len(uses))),
    ]
    if stream_vectors:
        scratch += [
            pltpu.VMEM((len(vectors), *vectors[0].shape), vectors[0].dtype),
            pltpu.SemaphoreType.DMA((len(vectors),)),
        ]
        vectors = [in_hbm(vector) for vector in vectors]
    return pl.pallas_call(
        kernel,
        out_shape=outs,
        in_specs=[hb if stream_vectors else vm] * len(vectors) + [hb] + [vm] * len(rest),
        out_specs=[vm] * len(outs),
        scratch_shapes=scratch,
        compiler_params=pltpu.CompilerParams(vmem_limit_bytes=VMEM_LIMIT),
        cost_estimate=pl.CostEstimate(
            flops=flops,
            bytes_accessed=2 * len(uses) * cols * height * width,
            transcendentals=0,
        ),
    )(*vectors, in_hbm(rows), *rest)


def body(t_upper, t_old, inverses, forcing, x_old, offsets, starts, column_map, z_cols, acc):
    n_col = lax.axis_size("col")
    n_row = lax.axis_size("row")
    row_idx = lax.axis_index("row")
    col_idx = lax.axis_index("col")
    steps, row_block, width = forcing.shape
    col_block = t_upper.shape[2]
    old_cols = x_old.shape[0]
    full_rows = col_block * n_col
    group = width // n_col
    share = row_block // n_col
    shape = jax.ShapeDtypeStruct

    def own_group(values):
        return lax.dynamic_slice_in_dim(values, col_idx * group, group, 0)

    gather = functools.partial(lax.all_gather, axis_name="col", axis=0)

    old_base = steps * full_rows + col_idx * old_cols
    (old_part,) = pl.pallas_call(
        old_kernel,
        out_shape=[
            shape((n_col, group, steps * row_block), F32),
        ],
        grid_spec=pltpu.PrefetchScalarGridSpec(
            num_scalar_prefetch=1,
            grid=(old_cols // CHUNK,),
            in_specs=[
                pl.BlockSpec((steps, row_block, CHUNK), lambda k, base: (0, 0, k)),
                pl.BlockSpec((CHUNK, width), lambda k, base: (k, 0)),
                pl.BlockSpec((1, width), lambda k, base: (0, 0)),
            ],
            out_specs=[
                pl.BlockSpec((n_col, group, steps * row_block), lambda k, base: (0, 0, 0)),
            ],
            scratch_shapes=[pltpu.VMEM((steps * row_block, width), F32)],
        ),
        compiler_params=pltpu.CompilerParams(vmem_limit_bytes=VMEM_LIMIT),
        cost_estimate=pl.CostEstimate(
            flops=2 * t_old.size * width, bytes_accessed=2 * t_old.size, transcendentals=0
        ),
    )(old_base[None], in_hbm(t_old), in_hbm(x_old), in_hbm(starts[None, :]))
    old_part, inverses = lax.optimization_barrier((old_part, inverses))
    gathered = {2: gather(inverses[2:3])}
    old_part = lax.all_to_all(old_part, "col", 0, 0)

    core = col_idx % 2
    my_starts = jnp.broadcast_to(own_group(starts)[:, None], (group, row_block))
    my_offsets = jnp.broadcast_to(own_group(offsets)[:, None], (group, row_block))
    forcing_t = lax.dynamic_slice_in_dim(
        forcing.reshape(steps * row_block, width), col_idx * group, group, 1
    ).T
    limits = [my_starts - (step * full_rows + row_idx * row_block) for step in range(steps)]
    order = jnp.arange(2 * width, dtype=jnp.int32)
    half_of = order // group % 2
    value_of = order // (2 * group) * group + order % group
    target = jnp.concatenate([column_map, column_map + width])
    hot = ((half_of * width + value_of)[:, None] == target[None, :]).astype(BF16)
    old_part, my_offsets, forcing_t, limits, hot, t_upper, inverses = lax.optimization_barrier(
        (old_part, my_offsets, forcing_t, limits, hot, t_upper, inverses)
    )
    gathered[1] = gather(jnp.concatenate([t_upper[2:3], inverses[1:2]]))
    which_inv = {2: 0, 1: 1, 0: 2}
    which_upper = {(1, 2): 0, (0, 1): 0, (0, 2): 1}

    send_shape = pltpu.VMEM((n_row, 2 * group, row_block), BF16)
    vec_shape = shape((group, row_block), F32)
    own_shape = pltpu.VMEM((2 * group, row_block), BF16)
    flops = 4 * group * row_block * full_rows

    def spread(send):
        return lax.all_to_all(send, "row", 0, 0)

    rest_shape = shape((group, (steps - 1) * row_block), F32)
    rhs_rest, send = call(first_kernel, [rest_shape, send_shape], old_part, forcing_t)
    early = list(range(1, steps))
    per = n_row // n_col
    z_rows = z_cols.shape[0]
    z_block = z_rows // n_col
    z_t = in_hbm(jnp.transpose(z_cols, (1, 0, 2)))
    z_params = pltpu.CompilerParams(vmem_limit_bytes=VMEM_LIMIT)
    mine = []
    everywhere = {}

    def cost(parts):
        return pl.CostEstimate(
            flops=4 * z_rows * parts * col_block * width,
            bytes_accessed=2 * z_rows * parts * col_block,
            transcendentals=0,
        )

    def early_z():
        gots = []
        for step in early:
            blocks = everywhere[step]
            gots.append(blocks)
            rows = lax.dynamic_index_in_dim(blocks, row_idx, 1, keepdims=False)
            mine.append(lax.dynamic_slice_in_dim(rows, col_idx * share, share, 2))
        tile = 2
        (out,) = pl.pallas_call(
            z_early_kernel,
            out_shape=[pltpu.HBM((n_col, z_block, width), F32)],
            grid_spec=pltpu.PrefetchScalarGridSpec(
                num_scalar_prefetch=1,
                grid=(n_col // tile,),
                in_specs=[
                    pl.BlockSpec(
                        (n_col, per, 2 * group, row_block), lambda i, place: (0, place[0], 0, 0)
                    )
                    for _ in gots
                ]
                + [
                    pl.BlockSpec(hot.shape, lambda i, place: (0, 0)),
                    pl.BlockSpec(
                        (pl.Element(steps - 1), pl.Element(tile * z_block), pl.Element(col_block)),
                        lambda i, place: (1, i * (tile * z_block), 0),
                    ),
                ],
                out_specs=[pl.BlockSpec((tile, z_block, width), lambda i, place: (i, 0, 0))],
                scratch_shapes=[pltpu.VMEM((steps - 1, col_block, 2 * width), BF16)],
            ),
            compiler_params=z_params,
            cost_estimate=cost(steps - 1),
        )(col_idx[None], *[in_hbm(got) for got in gots], hot, z_t)
        return out

    whole = {}
    own = {}
    for step in reversed(range(steps)):
        if step < steps - 1:
            later = range(step + 1, steps)
            uses = [which_upper[step, j] for j in later]
            (send,) = call_streamed(
                functools.partial(rhs_kernel, step, uses),
                uses,
                [send_shape],
                [whole[j] for j in later],
                gathered[step],
                [rhs_rest],
                stream_vectors=True,
                flops=flops * len(uses),
            )
        which = which_inv[step]
        rows = in_vmem(gathered[step])
        if step == steps - 1:
            send, total = call_streamed(
                functools.partial(first_streamed_kernel, which),
                [which],
                [send_shape, vec_shape],
                [spread(send)],
                gathered[step],
                flops=flops,
            )
            send, t_upper, inverses = lax.optimization_barrier((send, t_upper, inverses))
            gathered[0] = gather(jnp.concatenate([t_upper[:2], inverses[:1]]))
        else:
            send, total = call(
                functools.partial(first_term_kernel, which),
                [send_shape, vec_shape],
                spread(send),
                rows,
                flops=flops,
            )
        for extra in range(1, NEUMANN - 1):
            send, total = call(
                functools.partial(next_term_kernel, which),
                [send_shape, vec_shape],
                spread(send),
                rows,
                my_offsets,
                total,
                flops=flops,
            )
        send, own[step] = call(
            functools.partial(last_term_kernel, which),
            [send_shape, own_shape],
            spread(send),
            rows,
            my_offsets,
            total,
            limits[step],
            flops=flops,
        )
        if step == 0:
            own[0], everywhere = lax.optimization_barrier((own[0], everywhere))
        whole[step] = spread(send)
        if step > 0:
            everywhere[step] = gather(whole[step])
    whole[0], early_part = lax.optimization_barrier((whole[0], early_z()))

    (send,) = call(
        columns_kernel,
        [shape((n_col, 2 * group, col_block + LANES), BF16)],
        whole[0],
        own[0],
    )
    got = lax.all_to_all(send, "col", 0, 0)

    last = lax.dynamic_slice_in_dim(
        got, col_block + col_idx % (LANES // share) * share, share, 2
    )
    mine = jnp.stack([last] + mine).astype(F32)
    mine = mine[:, :, :group] + mine[:, :, group:]
    solved = jnp.transpose(mine, (0, 3, 1, 2)).reshape(steps, share, width)

    part_shape = shape((n_col // 2, z_block, width), F32)
    picked_shape = shape((col_block, 2 * width), BF16)
    in_vm = pl.BlockSpec(memory_space=pltpu.VMEM)
    in_hb = pl.BlockSpec(memory_space=pltpu.HBM)
    scalar = pl.BlockSpec(memory_space=pltpu.SMEM)
    scratch = [
        pltpu.VMEM((n_col // 2, z_block, col_block), BF16),
        pltpu.VMEM((n_col // 2, z_block, width), F32),
        pltpu.SemaphoreType.DMA((2, n_col // 2)),
    ]
    early_part = in_hbm(early_part)
    theirs, picked = pl.pallas_call(
        z_first_kernel,
        out_shape=[part_shape, picked_shape],
        in_specs=[scalar, in_vm, in_vm, in_hb, in_hb],
        out_specs=[in_vm, in_vm],
        scratch_shapes=scratch,
        compiler_params=z_params,
        cost_estimate=cost(1),
    )((1 - core)[None], got, hot, z_t, early_part)
    swapped = lax.ppermute(theirs, "col", [(i, i ^ 1) for i in range(n_col)])
    (ours,) = pl.pallas_call(
        z_next_kernel,
        out_shape=[part_shape],
        in_specs=[scalar, in_vm, in_hb, in_hb],
        out_specs=[in_vm],
        scratch_shapes=scratch,
        compiler_params=z_params,
        cost_estimate=cost(1),
    )(core[None], picked, z_t, early_part)
    part = lax.all_to_all(
        ours + swapped,
        "col",
        0,
        0,
        axis_index_groups=[list(range(c, n_col, 2)) for c in range(2)],
    )
    return (solved, acc + part.sum(0))


def solution(mesh):
    placed = (
        P(None, "row", "col"),
        P(None, "row", "col"),
        P(None, "row", "col"),
        P(None, "row", None),
        P("col", None),
        P(),
        P(),
        P(),
        P("row", None, "col"),
        P(("row", "col"), None),
    )
    return jax.shard_map(
        body,
        mesh=mesh,
        in_specs=placed,
        out_specs=(P(None, ("row", "col"), None), P(("row", "col"), None)),
        check_vma=False,
    )
```

```python
import functools

import jax
import jax.numpy as jnp
from jax import lax
from jax.experimental import pallas as pl
from jax.experimental.pallas import tpu as pltpu
from jax.sharding import PartitionSpec as P

NEUMANN = 3
F32 = jnp.float32
BF16 = jnp.bfloat16
VMEM_LIMIT = 16 << 20
LANES = 128
CHUNK = 1536


def rows_product(pairs_ref, rows_ref, which, copies=None):
    blocks, _, width = pairs_ref.shape
    per = blocks // rows_ref.shape[0]
    out = None
    for block in range(blocks):
        first = (block % per) * width
        if copies is not None and first == 0:
            copies[block // per].wait()
        part = lax.dot_general(
            pairs_ref[block],
            rows_ref[block // per, which, :, first : first + width],
            (((1,), (1,)), ((), ())),
            preferred_element_type=F32,
        )
        out = part if out is None else out + part
    half = out.shape[0] // 2
    return out[:half] + out[half:]


def pair_of(values):
    upper = values.astype(BF16)
    lower = (values - upper.astype(F32)).astype(BF16)
    return jnp.concatenate([upper, lower], axis=0)


def send_to_all(send_ref, pair):
    for peer in range(send_ref.shape[0]):
        send_ref[peer] = pair


def first_kernel(parts_ref, forcing_ref, rest_ref, send_ref):
    width = send_ref.shape[2]
    rhs = forcing_ref[...] - jnp.sum(parts_ref[...], axis=0)
    rest_ref[...] = rhs[:, :-width]
    send_to_all(send_ref, pair_of(rhs[:, -width:]))


def stream(rows_ref, uses, tiles_ref, sems):
    copies = []
    for k, which in enumerate(uses):
        copies.append(
            [
                pltpu.make_async_copy(rows_ref.at[j, which], tiles_ref.at[j, k], sems.at[j, k])
                for j in range(rows_ref.shape[0])
            ]
        )
        for copy in copies[-1]:
            copy.start()
    return copies


def rhs_kernel(step, uses, *refs):
    rows_ref, rhs_ref, send_ref, tiles_ref, sems, pairs_ref, pair_sems = refs[-7:]
    count = len(uses)
    firsts = [
        pltpu.make_async_copy(refs[k], pairs_ref.at[k], pair_sems.at[k]) for k in range(count)
    ]
    for copy in firsts:
        copy.start()
    copies = stream(rows_ref, uses, tiles_ref, sems)
    width = send_ref.shape[2]
    rhs = rhs_ref[:, step * width : (step + 1) * width]
    for k in range(count):
        firsts[k].wait()
        rhs = rhs - rows_product(pairs_ref.at[k], tiles_ref, k, copies[k])
    send_to_all(send_ref, pair_of(rhs))


def first_streamed_kernel(which, pairs_ref, rows_ref, send_ref, total_ref, tiles_ref, sems):
    copies = stream(rows_ref, [which], tiles_ref, sems)
    term = rows_product(pairs_ref, tiles_ref, 0, copies[0])
    total_ref[...] = term
    send_to_all(send_ref, pair_of(term))


def first_term_kernel(which, pairs_ref, rows_ref, send_ref, total_ref):
    term = rows_product(pairs_ref, rows_ref, which)
    total_ref[...] = term
    send_to_all(send_ref, pair_of(term))


def next_term_kernel(which, pairs_ref, rows_ref, scale_ref, old_ref, send_ref, total_ref):
    term = rows_product(pairs_ref, rows_ref, which) * scale_ref[...]
    total_ref[...] = old_ref[...] + term
    send_to_all(send_ref, pair_of(term))


def last_term_kernel(which, pairs_ref, rows_ref, scale_ref, old_ref, limit_ref, send_ref, own_ref):
    term = rows_product(pairs_ref, rows_ref, which) * scale_ref[...]
    total = old_ref[...] + term
    row = lax.broadcasted_iota(jnp.int32, total.shape, 1)
    pair = pair_of(jnp.where(row < limit_ref[...], total, 0.0))
    own_ref[...] = pair
    send_to_all(send_ref, pair)


def columns_kernel(whole_ref, own_ref, send_ref):
    n_col = send_ref.shape[0]
    blocks, _, width = whole_ref.shape
    per = blocks // n_col
    share = width // n_col
    for col in range(n_col):
        for k in range(per):
            send_ref[col, :, k * width : (k + 1) * width] = whole_ref[col * per + k]
        first = col * share // LANES * LANES
        send_ref[col, :, per * width :] = own_ref[:, first : first + LANES]


def pick(blocks, hot_ref):
    return lax.dot_general(
        jnp.concatenate(blocks, axis=0),
        hot_ref[...],
        (((0,), (0,)), ((), ())),
        preferred_element_type=F32,
    ).astype(BF16)


def fold(product):
    half = product.shape[1] // 2
    return product[:, :half] + product[:, half:]


def z_early_kernel(place_ref, *refs):
    hot_ref, z_ref, out_ref, picked_ref = refs[-4:]
    gots = refs[:-4]

    @pl.when(pl.program_id(0) == 0)
    def _():
        for k, got_ref in enumerate(gots):
            cols, per, _, width = got_ref.shape
            for j in range(per):
                blocks = [got_ref[col, j] for col in range(cols)]
                picked_ref[k, j * width : (j + 1) * width] = pick(blocks, hot_ref)

    out = None
    for k in range(len(gots)):
        part = jnp.dot(z_ref[k], picked_ref[k], preferred_element_type=F32)
        out = part if out is None else out + part
    out_ref[...] = fold(out).reshape(out_ref.shape)


def z_tiles(place_ref, z_ref, early_ref, tiles_ref, adds_ref, sems):
    copies = []
    count, size, _ = tiles_ref.shape
    for k in range(count):
        block = 2 * k + place_ref[0]
        rows = pl.ds(pl.multiple_of(block * size, size), size)
        copies.append(
            (
                pltpu.make_async_copy(z_ref.at[0, rows], tiles_ref.at[k], sems.at[0, k]),
                pltpu.make_async_copy(early_ref.at[block], adds_ref.at[k], sems.at[1, k]),
            )
        )
        for copy in copies[-1]:
            copy.start()
    return copies


def z_products(copies, picked, tiles_ref, adds_ref, out_ref):
    for k, both in enumerate(copies):
        for copy in both:
            copy.wait()
        product = jnp.dot(tiles_ref[k], picked, preferred_element_type=F32)
        out_ref[k] = adds_ref[k] + fold(product)


def z_first_kernel(
    place_ref, got_ref, hot_ref, z_ref, early_ref, out_ref, picked_ref, tiles_ref, adds_ref, sems
):
    copies = z_tiles(place_ref, z_ref, early_ref, tiles_ref, adds_ref, sems)
    depth = z_ref.shape[2]
    picked_ref[...] = pick([got_ref[k, :, :depth] for k in range(got_ref.shape[0])], hot_ref)
    z_products(copies, picked_ref[...], tiles_ref, adds_ref, out_ref)


def z_next_kernel(place_ref, picked_ref, z_ref, early_ref, out_ref, tiles_ref, adds_ref, sems):
    copies = z_tiles(place_ref, z_ref, early_ref, tiles_ref, adds_ref, sems)
    z_products(copies, picked_ref[...], tiles_ref, adds_ref, out_ref)


def old_kernel(base_ref, t_ref, old_ref, starts_ref, out_ref, sum_ref):
    k = pl.program_id(0)
    chunk = old_ref.shape[0]
    steps, rows, _ = t_ref.shape
    row = base_ref[0] + k * chunk + lax.broadcasted_iota(jnp.int32, old_ref.shape, 0)
    old = jnp.where(row < starts_ref[...], old_ref[...].astype(F32), 0.0).astype(BF16)
    t = t_ref[...].reshape(steps * rows, chunk)
    part = jnp.dot(t, old, preferred_element_type=F32)

    @pl.when(k == 0)
    def _():
        sum_ref[...] = part

    @pl.when(k > 0)
    def _():
        sum_ref[...] += part

    @pl.when(k == pl.num_programs(0) - 1)
    def _():
        group = out_ref.shape[1]
        whole = sum_ref[...].T
        for col in range(out_ref.shape[0]):
            out_ref[col] = whole[col * group : (col + 1) * group]


def call(kernel, outs, *args, flops=0):
    size = sum(a.size * a.dtype.itemsize for a in args)
    return pl.pallas_call(
        kernel,
        out_shape=outs,
        in_specs=[pl.BlockSpec(memory_space=pltpu.VMEM)] * len(args),
        out_specs=[pl.BlockSpec(memory_space=pltpu.VMEM)] * len(outs),
        compiler_params=pltpu.CompilerParams(vmem_limit_bytes=VMEM_LIMIT),
        cost_estimate=pl.CostEstimate(flops=flops, bytes_accessed=size, transcendentals=0),
    )(*args)


def in_vmem(values):
    return pltpu.with_memory_space_constraint(values, pltpu.VMEM)


def in_hbm(values):
    return pltpu.with_memory_space_constraint(values, pltpu.HBM)


def call_streamed(kernel, uses, outs, vectors, rows, rest=(), stream_vectors=False, flops=0):
    vm = pl.BlockSpec(memory_space=pltpu.VMEM)
    hb = pl.BlockSpec(memory_space=pltpu.HBM)
    cols, _, height, width = rows.shape
    scratch = [
        pltpu.VMEM((cols, len(uses), height, width), rows.dtype),
        pltpu.SemaphoreType.DMA((cols, len(uses))),
    ]
    if stream_vectors:
        scratch += [
            pltpu.VMEM((len(vectors), *vectors[0].shape), vectors[0].dtype),
            pltpu.SemaphoreType.DMA((len(vectors),)),
        ]
        vectors = [in_hbm(vector) for vector in vectors]
    return pl.pallas_call(
        kernel,
        out_shape=outs,
        in_specs=[hb if stream_vectors else vm] * len(vectors) + [hb] + [vm] * len(rest),
        out_specs=[vm] * len(outs),
        scratch_shapes=scratch,
        compiler_params=pltpu.CompilerParams(vmem_limit_bytes=VMEM_LIMIT),
        cost_estimate=pl.CostEstimate(
            flops=flops,
            bytes_accessed=2 * len(uses) * cols * height * width,
            transcendentals=0,
        ),
    )(*vectors, in_hbm(rows), *rest)


def body(t_upper, t_old, inverses, forcing, x_old, offsets, starts, column_map, z_cols, acc):
    n_col = lax.axis_size("col")
    n_row = lax.axis_size("row")
    row_idx = lax.axis_index("row")
    col_idx = lax.axis_index("col")
    steps, row_block, width = forcing.shape
    col_block = t_upper.shape[2]
    old_cols = x_old.shape[0]
    full_rows = col_block * n_col
    group = width // n_col
    share = row_block // n_col
    shape = jax.ShapeDtypeStruct

    def own_group(values):
        return lax.dynamic_slice_in_dim(values, col_idx * group, group, 0)

    gather = functools.partial(lax.all_gather, axis_name="col", axis=0)

    old_base = steps * full_rows + col_idx * old_cols
    (old_part,) = pl.pallas_call(
        old_kernel,
        out_shape=[
            shape((n_col, group, steps * row_block), F32),
        ],
        grid_spec=pltpu.PrefetchScalarGridSpec(
            num_scalar_prefetch=1,
            grid=(old_cols // CHUNK,),
            in_specs=[
                pl.BlockSpec((steps, row_block, CHUNK), lambda k, base: (0, 0, k)),
                pl.BlockSpec((CHUNK, width), lambda k, base: (k, 0)),
                pl.BlockSpec((1, width), lambda k, base: (0, 0)),
            ],
            out_specs=[
                pl.BlockSpec((n_col, group, steps * row_block), lambda k, base: (0, 0, 0)),
            ],
            scratch_shapes=[pltpu.VMEM((steps * row_block, width), F32)],
        ),
        compiler_params=pltpu.CompilerParams(vmem_limit_bytes=VMEM_LIMIT),
        cost_estimate=pl.CostEstimate(
            flops=2 * t_old.size * width, bytes_accessed=2 * t_old.size, transcendentals=0
        ),
    )(old_base[None], in_hbm(t_old), in_hbm(x_old), in_hbm(starts[None, :]))
    old_part, inverses = lax.optimization_barrier((old_part, inverses))
    gathered = {2: gather(inverses[2:3])}
    old_part = lax.all_to_all(old_part, "col", 0, 0)

    core = col_idx % 2
    my_starts = jnp.broadcast_to(own_group(starts)[:, None], (group, row_block))
    my_offsets = jnp.broadcast_to(own_group(offsets)[:, None], (group, row_block))
    forcing_t = lax.dynamic_slice_in_dim(
        forcing.reshape(steps * row_block, width), col_idx * group, group, 1
    ).T
    limits = [my_starts - (step * full_rows + row_idx * row_block) for step in range(steps)]
    order = jnp.arange(2 * width, dtype=jnp.int32)
    half_of = order // group % 2
    value_of = order // (2 * group) * group + order % group
    target = jnp.concatenate([column_map, column_map + width])
    hot = ((half_of * width + value_of)[:, None] == target[None, :]).astype(BF16)
    hot, t_upper, inverses = lax.optimization_barrier((hot, t_upper, inverses))
    set_b = jnp.concatenate([t_upper[2:3], inverses[1:2]])
    set_c = jnp.concatenate([t_upper[:2], inverses[:1]])
    old_part, my_offsets, forcing_t, limits, hot, set_b, set_c = lax.optimization_barrier(
        (old_part, my_offsets, forcing_t, limits, hot, set_b, set_c)
    )
    gathered[1] = gather(set_b)
    which_inv = {2: 0, 1: 1, 0: 2}
    which_upper = {(1, 2): 0, (0, 1): 0, (0, 2): 1}

    send_shape = pltpu.VMEM((n_row, 2 * group, row_block), BF16)
    vec_shape = shape((group, row_block), F32)
    own_shape = pltpu.VMEM((2 * group, row_block), BF16)
    flops = 4 * group * row_block * full_rows

    def spread(send):
        return lax.all_to_all(send, "row", 0, 0)

    rest_shape = shape((group, (steps - 1) * row_block), F32)
    rhs_rest, send = call(first_kernel, [rest_shape, send_shape], old_part, forcing_t)
    early = list(range(1, steps))
    per = n_row // n_col
    z_rows = z_cols.shape[0]
    z_block = z_rows // n_col
    z_t = in_hbm(jnp.transpose(z_cols, (1, 0, 2)))
    z_params = pltpu.CompilerParams(vmem_limit_bytes=VMEM_LIMIT)
    mine = []
    everywhere = {}

    def cost(parts):
        return pl.CostEstimate(
            flops=4 * z_rows * parts * col_block * width,
            bytes_accessed=2 * z_rows * parts * col_block,
            transcendentals=0,
        )

    def early_z():
        gots = []
        for step in early:
            blocks = everywhere[step]
            gots.append(blocks)
            rows = lax.dynamic_index_in_dim(blocks, row_idx, 1, keepdims=False)
            mine.append(lax.dynamic_slice_in_dim(rows, col_idx * share, share, 2))
        tile = 2
        (out,) = pl.pallas_call(
            z_early_kernel,
            out_shape=[pltpu.HBM((n_col, z_block, width), F32)],
            grid_spec=pltpu.PrefetchScalarGridSpec(
                num_scalar_prefetch=1,
                grid=(n_col // tile,),
                in_specs=[
                    pl.BlockSpec(
                        (n_col, per, 2 * group, row_block), lambda i, place: (0, place[0], 0, 0)
                    )
                    for _ in gots
                ]
                + [
                    pl.BlockSpec(hot.shape, lambda i, place: (0, 0)),
                    pl.BlockSpec(
                        (pl.Element(steps - 1), pl.Element(tile * z_block), pl.Element(col_block)),
                        lambda i, place: (1, i * (tile * z_block), 0),
                    ),
                ],
                out_specs=[pl.BlockSpec((tile, z_block, width), lambda i, place: (i, 0, 0))],
                scratch_shapes=[pltpu.VMEM((steps - 1, col_block, 2 * width), BF16)],
            ),
            compiler_params=z_params,
            cost_estimate=cost(steps - 1),
        )(col_idx[None], *[in_hbm(got) for got in gots], hot, z_t)
        return out

    whole = {}
    own = {}
    for step in reversed(range(steps)):
        if step < steps - 1:
            later = range(step + 1, steps)
            uses = [which_upper[step, j] for j in later]
            (send,) = call_streamed(
                functools.partial(rhs_kernel, step, uses),
                uses,
                [send_shape],
                [whole[j] for j in later],
                gathered[step],
                [rhs_rest],
                stream_vectors=True,
                flops=flops * len(uses),
            )
        which = which_inv[step]
        rows = in_vmem(gathered[step])
        if step == steps - 1:
            send, total = call_streamed(
                functools.partial(first_streamed_kernel, which),
                [which],
                [send_shape, vec_shape],
                [spread(send)],
                gathered[step],
                flops=flops,
            )
            send, set_c = lax.optimization_barrier((send, set_c))
            gathered[0] = gather(set_c)
        else:
            send, total = call(
                functools.partial(first_term_kernel, which),
                [send_shape, vec_shape],
                spread(send),
                rows,
                flops=flops,
            )
        for extra in range(1, NEUMANN - 1):
            send, total = call(
                functools.partial(next_term_kernel, which),
                [send_shape, vec_shape],
                spread(send),
                rows,
                my_offsets,
                total,
                flops=flops,
            )
        send, own[step] = call(
            functools.partial(last_term_kernel, which),
            [send_shape, own_shape],
            spread(send),
            rows,
            my_offsets,
            total,
            limits[step],
            flops=flops,
        )
        if step == 0:
            own[0], everywhere = lax.optimization_barrier((own[0], everywhere))
        whole[step] = spread(send)
        if step > 0:
            everywhere[step] = gather(whole[step])
    whole[0], early_part = lax.optimization_barrier((whole[0], early_z()))

    (send,) = call(
        columns_kernel,
        [shape((n_col, 2 * group, col_block + LANES), BF16)],
        whole[0],
        own[0],
    )
    got = lax.all_to_all(send, "col", 0, 0)

    last = lax.dynamic_slice_in_dim(
        got, col_block + col_idx % (LANES // share) * share, share, 2
    )
    mine = jnp.stack([last] + mine).astype(F32)
    mine = mine[:, :, :group] + mine[:, :, group:]
    solved = jnp.transpose(mine, (0, 3, 1, 2)).reshape(steps, share, width)

    part_shape = shape((n_col // 2, z_block, width), F32)
    picked_shape = shape((col_block, 2 * width), BF16)
    in_vm = pl.BlockSpec(memory_space=pltpu.VMEM)
    in_hb = pl.BlockSpec(memory_space=pltpu.HBM)
    scalar = pl.BlockSpec(memory_space=pltpu.SMEM)
    scratch = [
        pltpu.VMEM((n_col // 2, z_block, col_block), BF16),
        pltpu.VMEM((n_col // 2, z_block, width), F32),
        pltpu.SemaphoreType.DMA((2, n_col // 2)),
    ]
    early_part = in_hbm(early_part)
    theirs, picked = pl.pallas_call(
        z_first_kernel,
        out_shape=[part_shape, picked_shape],
        in_specs=[scalar, in_vm, in_vm, in_hb, in_hb],
        out_specs=[in_vm, in_vm],
        scratch_shapes=scratch,
        compiler_params=z_params,
        cost_estimate=cost(1),
    )((1 - core)[None], got, hot, z_t, early_part)
    swapped = lax.ppermute(theirs, "col", [(i, i ^ 1) for i in range(n_col)])
    (ours,) = pl.pallas_call(
        z_next_kernel,
        out_shape=[part_shape],
        in_specs=[scalar, in_vm, in_hb, in_hb],
        out_specs=[in_vm],
        scratch_shapes=scratch,
        compiler_params=z_params,
        cost_estimate=cost(1),
    )(core[None], picked, z_t, early_part)
    part = lax.all_to_all(
        ours + swapped,
        "col",
        0,
        0,
        axis_index_groups=[list(range(c, n_col, 2)) for c in range(2)],
    )
    return (solved, acc + part.sum(0))


def solution(mesh):
    placed = (
        P(None, "row", "col"),
        P(None, "row", "col"),
        P(None, "row", "col"),
        P(None, "row", None),
        P("col", None),
        P(),
        P(),
        P(),
        P("row", None, "col"),
        P(("row", "col"), None),
    )
    return jax.shard_map(
        body,
        mesh=mesh,
        in_specs=placed,
        out_specs=(P(None, ("row", "col"), None), P(("row", "col"), None)),
        check_vma=False,
    )
```

```python
import functools

import jax
import jax.numpy as jnp
from jax import lax
from jax.experimental import pallas as pl
from jax.experimental.pallas import tpu as pltpu
from jax.sharding import PartitionSpec as P

NEUMANN = 3
F32 = jnp.float32
BF16 = jnp.bfloat16
VMEM_LIMIT = 16 << 20
LANES = 128
CHUNK = 1536


def rows_product(pairs_ref, rows_ref, which, copies=None):
    blocks, _, width = pairs_ref.shape
    per = blocks // rows_ref.shape[0]
    out = None
    for block in range(blocks):
        first = (block % per) * width
        if copies is not None and first == 0:
            copies[block // per].wait()
        part = lax.dot_general(
            pairs_ref[block],
            rows_ref[block // per, which, :, first : first + width],
            (((1,), (1,)), ((), ())),
            preferred_element_type=F32,
        )
        out = part if out is None else out + part
    half = out.shape[0] // 2
    return out[:half] + out[half:]


def pair_of(values):
    upper = values.astype(BF16)
    lower = (values - upper.astype(F32)).astype(BF16)
    return jnp.concatenate([upper, lower], axis=0)


def send_to_all(send_ref, pair):
    for peer in range(send_ref.shape[0]):
        send_ref[peer] = pair


def first_kernel(parts_ref, forcing_ref, rest_ref, send_ref):
    width = send_ref.shape[2]
    rhs = forcing_ref[...] - jnp.sum(parts_ref[...], axis=0)
    rest_ref[...] = rhs[:, :-width]
    send_to_all(send_ref, pair_of(rhs[:, -width:]))


def stream(rows_ref, uses, tiles_ref, sems):
    copies = []
    for k, which in enumerate(uses):
        copies.append(
            [
                pltpu.make_async_copy(rows_ref.at[j, which], tiles_ref.at[j, k], sems.at[j, k])
                for j in range(rows_ref.shape[0])
            ]
        )
        for copy in copies[-1]:
            copy.start()
    return copies


def rhs_kernel(step, uses, *refs):
    rows_ref, rhs_ref, send_ref, tiles_ref, sems, pairs_ref, pair_sems = refs[-7:]
    count = len(uses)
    firsts = [
        pltpu.make_async_copy(refs[k], pairs_ref.at[k], pair_sems.at[k]) for k in range(count)
    ]
    for copy in firsts:
        copy.start()
    copies = stream(rows_ref, uses, tiles_ref, sems)
    width = send_ref.shape[2]
    rhs = rhs_ref[:, step * width : (step + 1) * width]
    for k in range(count):
        firsts[k].wait()
        rhs = rhs - rows_product(pairs_ref.at[k], tiles_ref, k, copies[k])
    send_to_all(send_ref, pair_of(rhs))


def first_streamed_kernel(which, pairs_ref, rows_ref, send_ref, total_ref, tiles_ref, sems):
    copies = stream(rows_ref, [which], tiles_ref, sems)
    term = rows_product(pairs_ref, tiles_ref, 0, copies[0])
    total_ref[...] = term
    send_to_all(send_ref, pair_of(term))


def first_term_kernel(which, pairs_ref, rows_ref, send_ref, total_ref):
    term = rows_product(pairs_ref, rows_ref, which)
    total_ref[...] = term
    send_to_all(send_ref, pair_of(term))


def next_term_kernel(which, pairs_ref, rows_ref, scale_ref, old_ref, send_ref, total_ref):
    term = rows_product(pairs_ref, rows_ref, which) * scale_ref[...]
    total_ref[...] = old_ref[...] + term
    send_to_all(send_ref, pair_of(term))


def last_term_kernel(which, pairs_ref, rows_ref, scale_ref, old_ref, limit_ref, send_ref, *own_ref):
    term = rows_product(pairs_ref, rows_ref, which) * scale_ref[...]
    total = old_ref[...] + term
    row = lax.broadcasted_iota(jnp.int32, total.shape, 1)
    pair = pair_of(jnp.where(row < limit_ref[...], total, 0.0))
    if own_ref:
        own_ref[0][...] = pair
    send_to_all(send_ref, pair)


def columns_kernel(whole_ref, own_ref, send_ref):
    n_col = send_ref.shape[0]
    blocks, _, width = whole_ref.shape
    per = blocks // n_col
    share = width // n_col
    for col in range(n_col):
        for k in range(per):
            send_ref[col, :, k * width : (k + 1) * width] = whole_ref[col * per + k]
        first = col * share // LANES * LANES
        send_ref[col, :, per * width :] = own_ref[:, first : first + LANES]


def pick(blocks, hot_ref):
    return lax.dot_general(
        jnp.concatenate(blocks, axis=0),
        hot_ref[...],
        (((0,), (0,)), ((), ())),
        preferred_element_type=F32,
    ).astype(BF16)


def fold(product):
    half = product.shape[1] // 2
    return product[:, :half] + product[:, half:]


def z_early_kernel(place_ref, *refs):
    hot_ref, z_ref, out_ref, picked_ref = refs[-4:]
    gots = refs[:-4]

    @pl.when(pl.program_id(0) == 0)
    def _():
        for k, got_ref in enumerate(gots):
            cols, per, _, width = got_ref.shape
            for j in range(per):
                blocks = [got_ref[col, j] for col in range(cols)]
                picked_ref[k, j * width : (j + 1) * width] = pick(blocks, hot_ref)

    out = None
    for k in range(len(gots)):
        part = jnp.dot(z_ref[k], picked_ref[k], preferred_element_type=F32)
        out = part if out is None else out + part
    out_ref[...] = fold(out).reshape(out_ref.shape)


def z_tiles(place_ref, z_ref, early_ref, tiles_ref, adds_ref, sems):
    copies = []
    count, size, _ = tiles_ref.shape
    for k in range(count):
        block = 2 * k + place_ref[0]
        rows = pl.ds(pl.multiple_of(block * size, size), size)
        copies.append(
            (
                pltpu.make_async_copy(z_ref.at[0, rows], tiles_ref.at[k], sems.at[0, k]),
                pltpu.make_async_copy(early_ref.at[block], adds_ref.at[k], sems.at[1, k]),
            )
        )
        for copy in copies[-1]:
            copy.start()
    return copies


def z_products(copies, picked, tiles_ref, adds_ref, out_ref):
    for k, both in enumerate(copies):
        for copy in both:
            copy.wait()
        product = jnp.dot(tiles_ref[k], picked, preferred_element_type=F32)
        out_ref[k] = adds_ref[k] + fold(product)


def z_first_kernel(
    place_ref, got_ref, hot_ref, z_ref, early_ref, out_ref, picked_ref, tiles_ref, adds_ref, sems
):
    copies = z_tiles(place_ref, z_ref, early_ref, tiles_ref, adds_ref, sems)
    depth = z_ref.shape[2]
    picked_ref[...] = pick([got_ref[k, :, :depth] for k in range(got_ref.shape[0])], hot_ref)
    z_products(copies, picked_ref[...], tiles_ref, adds_ref, out_ref)


def z_next_kernel(place_ref, picked_ref, z_ref, early_ref, out_ref, tiles_ref, adds_ref, sems):
    copies = z_tiles(place_ref, z_ref, early_ref, tiles_ref, adds_ref, sems)
    z_products(copies, picked_ref[...], tiles_ref, adds_ref, out_ref)


def old_kernel(base_ref, t_ref, old_ref, starts_ref, out_ref, sum_ref):
    k = pl.program_id(0)
    chunk = old_ref.shape[0]
    steps, rows, _ = t_ref.shape
    row = base_ref[0] + k * chunk + lax.broadcasted_iota(jnp.int32, old_ref.shape, 0)
    old = jnp.where(row < starts_ref[...], old_ref[...].astype(F32), 0.0).astype(BF16)
    t = t_ref[...].reshape(steps * rows, chunk)
    part = jnp.dot(t, old, preferred_element_type=F32)

    @pl.when(k == 0)
    def _():
        sum_ref[...] = part

    @pl.when(k > 0)
    def _():
        sum_ref[...] += part

    @pl.when(k == pl.num_programs(0) - 1)
    def _():
        group = out_ref.shape[1]
        whole = sum_ref[...].T
        for col in range(out_ref.shape[0]):
            out_ref[col] = whole[col * group : (col + 1) * group]


def call(kernel, outs, *args, flops=0):
    size = sum(a.size * a.dtype.itemsize for a in args)
    return pl.pallas_call(
        kernel,
        out_shape=outs,
        in_specs=[pl.BlockSpec(memory_space=pltpu.VMEM)] * len(args),
        out_specs=[pl.BlockSpec(memory_space=pltpu.VMEM)] * len(outs),
        compiler_params=pltpu.CompilerParams(vmem_limit_bytes=VMEM_LIMIT),
        cost_estimate=pl.CostEstimate(flops=flops, bytes_accessed=size, transcendentals=0),
    )(*args)


def in_vmem(values):
    return pltpu.with_memory_space_constraint(values, pltpu.VMEM)


def in_hbm(values):
    return pltpu.with_memory_space_constraint(values, pltpu.HBM)


def call_streamed(kernel, uses, outs, vectors, rows, rest=(), stream_vectors=False, flops=0):
    vm = pl.BlockSpec(memory_space=pltpu.VMEM)
    hb = pl.BlockSpec(memory_space=pltpu.HBM)
    cols, _, height, width = rows.shape
    scratch = [
        pltpu.VMEM((cols, len(uses), height, width), rows.dtype),
        pltpu.SemaphoreType.DMA((cols, len(uses))),
    ]
    if stream_vectors:
        scratch += [
            pltpu.VMEM((len(vectors), *vectors[0].shape), vectors[0].dtype),
            pltpu.SemaphoreType.DMA((len(vectors),)),
        ]
        vectors = [in_hbm(vector) for vector in vectors]
    return pl.pallas_call(
        kernel,
        out_shape=outs,
        in_specs=[hb if stream_vectors else vm] * len(vectors) + [hb] + [vm] * len(rest),
        out_specs=[vm] * len(outs),
        scratch_shapes=scratch,
        compiler_params=pltpu.CompilerParams(vmem_limit_bytes=VMEM_LIMIT),
        cost_estimate=pl.CostEstimate(
            flops=flops,
            bytes_accessed=2 * len(uses) * cols * height * width,
            transcendentals=0,
        ),
    )(*vectors, in_hbm(rows), *rest)


def body(t_upper, t_old, inverses, forcing, x_old, offsets, starts, column_map, z_cols, acc):
    n_col = lax.axis_size("col")
    n_row = lax.axis_size("row")
    row_idx = lax.axis_index("row")
    col_idx = lax.axis_index("col")
    steps, row_block, width = forcing.shape
    col_block = t_upper.shape[2]
    old_cols = x_old.shape[0]
    full_rows = col_block * n_col
    group = width // n_col
    share = row_block // n_col
    shape = jax.ShapeDtypeStruct

    def own_group(values):
        return lax.dynamic_slice_in_dim(values, col_idx * group, group, 0)

    gather = functools.partial(lax.all_gather, axis_name="col", axis=0)

    old_base = steps * full_rows + col_idx * old_cols
    (old_part,) = pl.pallas_call(
        old_kernel,
        out_shape=[
            shape((n_col, group, steps * row_block), F32),
        ],
        grid_spec=pltpu.PrefetchScalarGridSpec(
            num_scalar_prefetch=1,
            grid=(old_cols // CHUNK,),
            in_specs=[
                pl.BlockSpec((steps, row_block, CHUNK), lambda k, base: (0, 0, k)),
                pl.BlockSpec((CHUNK, width), lambda k, base: (k, 0)),
                pl.BlockSpec((1, width), lambda k, base: (0, 0)),
            ],
            out_specs=[
                pl.BlockSpec((n_col, group, steps * row_block), lambda k, base: (0, 0, 0)),
            ],
            scratch_shapes=[pltpu.VMEM((steps * row_block, width), F32)],
        ),
        compiler_params=pltpu.CompilerParams(vmem_limit_bytes=VMEM_LIMIT),
        cost_estimate=pl.CostEstimate(
            flops=2 * t_old.size * width, bytes_accessed=2 * t_old.size, transcendentals=0
        ),
    )(old_base[None], in_hbm(t_old), in_hbm(x_old), in_hbm(starts[None, :]))
    old_part, inverses = lax.optimization_barrier((old_part, inverses))
    gathered = {2: gather(inverses[2:3])}
    old_part = lax.all_to_all(old_part, "col", 0, 0)

    core = col_idx % 2
    my_starts = jnp.broadcast_to(own_group(starts)[:, None], (group, row_block))
    my_offsets = jnp.broadcast_to(own_group(offsets)[:, None], (group, row_block))
    forcing_t = lax.dynamic_slice_in_dim(
        forcing.reshape(steps * row_block, width), col_idx * group, group, 1
    ).T
    limits = [my_starts - (step * full_rows + row_idx * row_block) for step in range(steps)]
    order = jnp.arange(2 * width, dtype=jnp.int32)
    half_of = order // group % 2
    value_of = order // (2 * group) * group + order % group
    target = jnp.concatenate([column_map, column_map + width])
    hot = ((half_of * width + value_of)[:, None] == target[None, :]).astype(BF16)
    hot, t_upper, inverses = lax.optimization_barrier((hot, t_upper, inverses))
    set_b = jnp.concatenate([t_upper[2:3], inverses[1:2]])
    set_c = jnp.concatenate([t_upper[:2], inverses[:1]])
    old_part, my_offsets, forcing_t, limits, hot, set_b, set_c = lax.optimization_barrier(
        (old_part, my_offsets, forcing_t, limits, hot, set_b, set_c)
    )
    gathered[1] = gather(set_b)
    which_inv = {2: 0, 1: 1, 0: 2}
    which_upper = {(1, 2): 0, (0, 1): 0, (0, 2): 1}

    send_shape = pltpu.VMEM((n_row, 2 * group, row_block), BF16)
    vec_shape = shape((group, row_block), F32)
    own_shape = pltpu.VMEM((2 * group, row_block), BF16)
    flops = 4 * group * row_block * full_rows

    def spread(send):
        return lax.all_to_all(send, "row", 0, 0)

    rest_shape = shape((group, (steps - 1) * row_block), F32)
    rhs_rest, send = call(first_kernel, [rest_shape, send_shape], old_part, forcing_t)
    early = list(range(1, steps))
    per = n_row // n_col
    z_rows = z_cols.shape[0]
    z_block = z_rows // n_col
    z_t = in_hbm(jnp.transpose(z_cols, (1, 0, 2)))
    z_params = pltpu.CompilerParams(vmem_limit_bytes=VMEM_LIMIT)
    mine = []
    everywhere = {}

    def cost(parts):
        return pl.CostEstimate(
            flops=4 * z_rows * parts * col_block * width,
            bytes_accessed=2 * z_rows * parts * col_block,
            transcendentals=0,
        )

    def early_z():
        gots = []
        for step in early:
            blocks = everywhere[step]
            gots.append(blocks)
            rows = lax.dynamic_index_in_dim(blocks, row_idx, 1, keepdims=False)
            mine.append(lax.dynamic_slice_in_dim(rows, col_idx * share, share, 2))
        tile = 2
        (out,) = pl.pallas_call(
            z_early_kernel,
            out_shape=[pltpu.HBM((n_col, z_block, width), F32)],
            grid_spec=pltpu.PrefetchScalarGridSpec(
                num_scalar_prefetch=1,
                grid=(n_col // tile,),
                in_specs=[
                    pl.BlockSpec(
                        (n_col, per, 2 * group, row_block), lambda i, place: (0, place[0], 0, 0)
                    )
                    for _ in gots
                ]
                + [
                    pl.BlockSpec(hot.shape, lambda i, place: (0, 0)),
                    pl.BlockSpec(
                        (pl.Element(steps - 1), pl.Element(tile * z_block), pl.Element(col_block)),
                        lambda i, place: (1, i * (tile * z_block), 0),
                    ),
                ],
                out_specs=[pl.BlockSpec((tile, z_block, width), lambda i, place: (i, 0, 0))],
                scratch_shapes=[pltpu.VMEM((steps - 1, col_block, 2 * width), BF16)],
            ),
            compiler_params=z_params,
            cost_estimate=cost(steps - 1),
        )(col_idx[None], *[in_hbm(got) for got in gots], hot, z_t)
        return out

    whole = {}
    own = {}
    for step in reversed(range(steps)):
        if step < steps - 1:
            later = range(step + 1, steps)
            uses = [which_upper[step, j] for j in later]
            (send,) = call_streamed(
                functools.partial(rhs_kernel, step, uses),
                uses,
                [send_shape],
                [whole[j] for j in later],
                gathered[step],
                [rhs_rest],
                stream_vectors=True,
                flops=flops * len(uses),
            )
        which = which_inv[step]
        rows = in_vmem(gathered[step])
        if step == steps - 1:
            send, total = call_streamed(
                functools.partial(first_streamed_kernel, which),
                [which],
                [send_shape, vec_shape],
                [spread(send)],
                gathered[step],
                flops=flops,
            )
            send, set_c = lax.optimization_barrier((send, set_c))
            gathered[0] = gather(set_c)
        else:
            send, total = call(
                functools.partial(first_term_kernel, which),
                [send_shape, vec_shape],
                spread(send),
                rows,
                flops=flops,
            )
        for extra in range(1, NEUMANN - 1):
            send, total = call(
                functools.partial(next_term_kernel, which),
                [send_shape, vec_shape],
                spread(send),
                rows,
                my_offsets,
                total,
                flops=flops,
            )
        send, *own[step] = call(
            functools.partial(last_term_kernel, which),
            [send_shape] if step else [send_shape, own_shape],
            spread(send),
            rows,
            my_offsets,
            total,
            limits[step],
            flops=flops,
        )
        if step == 0:
            own[0], everywhere = lax.optimization_barrier((own[0][0], everywhere))
        whole[step] = spread(send)
        if step > 0:
            everywhere[step] = gather(whole[step])
    whole[0], early_part = lax.optimization_barrier((whole[0], early_z()))

    (send,) = call(
        columns_kernel,
        [shape((n_col, 2 * group, col_block + LANES), BF16)],
        whole[0],
        own[0],
    )
    got = lax.all_to_all(send, "col", 0, 0)

    last = lax.dynamic_slice_in_dim(
        got, col_block + col_idx % (LANES // share) * share, share, 2
    )
    mine = jnp.stack([last] + mine).astype(F32)
    mine = mine[:, :, :group] + mine[:, :, group:]
    solved = jnp.transpose(mine, (0, 3, 1, 2)).reshape(steps, share, width)

    part_shape = shape((n_col // 2, z_block, width), F32)
    picked_shape = shape((col_block, 2 * width), BF16)
    in_vm = pl.BlockSpec(memory_space=pltpu.VMEM)
    in_hb = pl.BlockSpec(memory_space=pltpu.HBM)
    scalar = pl.BlockSpec(memory_space=pltpu.SMEM)
    scratch = [
        pltpu.VMEM((n_col // 2, z_block, col_block), BF16),
        pltpu.VMEM((n_col // 2, z_block, width), F32),
        pltpu.SemaphoreType.DMA((2, n_col // 2)),
    ]
    early_part = in_hbm(early_part)
    theirs, picked = pl.pallas_call(
        z_first_kernel,
        out_shape=[part_shape, picked_shape],
        in_specs=[scalar, in_vm, in_vm, in_hb, in_hb],
        out_specs=[in_vm, in_vm],
        scratch_shapes=scratch,
        compiler_params=z_params,
        cost_estimate=cost(1),
    )((1 - core)[None], got, hot, z_t, early_part)
    swapped = lax.ppermute(theirs, "col", [(i, i ^ 1) for i in range(n_col)])
    (ours,) = pl.pallas_call(
        z_next_kernel,
        out_shape=[part_shape],
        in_specs=[scalar, in_vm, in_hb, in_hb],
        out_specs=[in_vm],
        scratch_shapes=scratch,
        compiler_params=z_params,
        cost_estimate=cost(1),
    )(core[None], picked, z_t, early_part)
    part = lax.all_to_all(
        ours + swapped,
        "col",
        0,
        0,
        axis_index_groups=[list(range(c, n_col, 2)) for c in range(2)],
    )
    return (solved, acc + part.sum(0))


def solution(mesh):
    placed = (
        P(None, "row", "col"),
        P(None, "row", "col"),
        P(None, "row", "col"),
        P(None, "row", None),
        P("col", None),
        P(),
        P(),
        P(),
        P("row", None, "col"),
        P(("row", "col"), None),
    )
    return jax.shard_map(
        body,
        mesh=mesh,
        in_specs=placed,
        out_specs=(P(None, ("row", "col"), None), P(("row", "col"), None)),
        check_vma=False,
    )
```
